32 devices in a mesh: src: 8 (over z, core), tgt: 4 (over y, x).
Axes of the slice: x: 2, y: 2, z: 4, core: 2. Of those that a mesh axis runs over, the one named last changes fastest.
Arguments:
- charges: bfloat16 [65536, 64], P(('src', 'tgt')), may hold values from -6 to 6
- near_tiles: bfloat16 [4096, 128, 128], P(('src', 'tgt')), may hold values from -0.0625 to 0.0625
- near_tgt: int32 [4096], P(('src', 'tgt')), may hold values from 0 to 127
- near_src: int32 [4096], P(('src', 'tgt')), may hold values from 0 to 15
- leaf_basis: bfloat16 [512, 64, 128], P(('src', 'tgt')), may hold values from -0.125 to 0.125
- transfer: float32 [8, 3, 64, 128], P('src'), may hold values from -0.5 to 0.5
- coupling: bfloat16 [8, 512, 64, 256], P('src', 'tgt'), may hold values from -0.375 to 0.375
- far_node: int32 [8, 512, 4], P('src', 'tgt'), may hold values from 0 to 6
- target_basis: bfloat16 [512, 64, 128], P('tgt'), may hold values from -0.25 to 0.25
Outputs:
- potential: bfloat16 [65536, 64], P('tgt')
The draws below stay inside these ranges and needn't reach their ends.
All inputs are finite; a program needn't handle non-finite values.
Results may differ from the reference program's by a relative error of at most 0.0057.
Values may be sent and summed in bfloat16 or wider, within the bound.
No kernel may reach another device: no remote copies, remote signals or barrier semaphores. Data moves between devices by JAX's collectives and lax.ppermute only.
A program may use at most 128 MiB of HBM per device.

```python
import jax
import jax.numpy as jnp
from jax import lax

TILE = 128
RANK = 64
NRHS = 64
SRC_TILES_DEV = 16
NEAR_DEV = 128
FAR_PER = 4
TGT_TILES_DEV = 128
SLOTS = 32
NODES = 7
SRC_TILES = 512
TGT_TILES = 512
NEAR_ALL = 4096
N_SRC = 8
N_TGT = 4


def place_ends(drawn, own_key, smallest, top_value):
    longest = drawn.shape.index(max(drawn.shape))
    spots = []
    for shift in (0, 1):
        where = [jax.random.randint(jax.random.fold_in(own_key, axis), (), 0, length) for axis, length in enumerate(drawn.shape)]
        where[longest] = (where[longest] + shift) % drawn.shape[longest]
        spots.append(tuple(where))
    return drawn.at[spots[0]].set(smallest).at[spots[1]].set(top_value)


def level_of(key, extent, split, smallest, largest):
    loudness, own = 1.0, jax.random.fold_in(key, 6)
    for dim, shards_of in split:
        heights = jnp.exp(jax.random.uniform(jax.random.fold_in(own, dim), (shards_of,), jnp.float32, smallest / len(split), largest / len(split)))
        loudness = loudness * jnp.repeat(heights, extent[dim] // shards_of).reshape([-1 if axis == dim else 1 for axis in range(len(extent))])
    return loudness


def normal_values(rng, dims, spread, limit, cuts=(), held_as=jnp.bfloat16):
    values = jax.random.normal(rng, dims, jnp.float32) * spread
    if len(cuts) > 0:
        values = level_of(rng, dims, cuts, -0.22, 0.18) * values
    return jnp.clip(values, min=-limit, max=limit).astype(held_as)


def setup_inputs(seed: int = 0) -> dict:
    keys = jax.random.split(jax.random.key(seed), 10)
    charges = normal_values(keys[0], (SRC_TILES * TILE, NRHS), 1.0, 6.0, ((0, 32),))
    near_tiles = normal_values(keys[1], (NEAR_ALL, TILE, TILE), (TILE * 64) ** -0.5, 0.0625, ((0, 32),))
    near_tgt = place_ends(jax.random.randint(keys[2], (NEAR_ALL,), 0, TGT_TILES_DEV), jax.random.fold_in(keys[2], 1), 0, TGT_TILES_DEV - 1).astype(jnp.int32)
    near_src = place_ends(jax.random.randint(keys[3], (NEAR_ALL,), 0, SRC_TILES_DEV), jax.random.fold_in(keys[3], 1), 0, SRC_TILES_DEV - 1).astype(jnp.int32)
    leaf_basis = normal_values(keys[4], (SRC_TILES, RANK, TILE), (TILE * SRC_TILES_DEV) ** -0.5, 0.125, ((0, 32),))
    transfer = normal_values(keys[5], (N_SRC, N_TGT - 1, RANK, 2 * RANK), (2 * RANK) ** -0.5, 0.5, ((0, 8),), jnp.float32)
    coupling = normal_values(keys[6], (N_SRC, TGT_TILES, RANK, FAR_PER * RANK), (RANK * FAR_PER) ** -0.5, 0.375, ((0, 8), (1, 4)))
    far_node = place_ends(jax.random.randint(keys[7], (N_SRC, TGT_TILES, FAR_PER), 0, NODES), jax.random.fold_in(keys[7], 1), 0, NODES - 1).astype(jnp.int32)
    target_basis = normal_values(keys[8], (TGT_TILES, RANK, TILE), (RANK * N_SRC) ** -0.5, 0.25, ((0, 4),))
    return {"charges": charges, "near_tiles": near_tiles, "near_tgt": near_tgt, "near_src": near_src, "leaf_basis": leaf_basis, "transfer": transfer, "coupling": coupling, "far_node": far_node, "target_basis": target_basis}


def climb(edges, leaves):
    levels = [leaves]
    level = leaves
    width = leaves.shape[0]
    while width > 1:
        width = width // 2
        edge_slab = edges[width - 1:2 * width - 1]
        pairs = level.reshape(width, 2 * level.shape[1], level.shape[2])
        level = jnp.einsum('prc,pcn->prn', edge_slab, pairs, precision=lax.Precision.HIGHEST)
        levels.insert(0, level)
    return jnp.concatenate(levels, axis=0)


def reference(charges, near_tiles, near_tgt, near_src, leaf_basis, transfer, coupling, far_node, target_basis):
    leaf_charges = charges.astype(jnp.float32).reshape(SRC_TILES, TILE, NRHS)
    dest_block = (jnp.arange(NEAR_DEV) // SLOTS).astype(jnp.int32)

    def near_step(accum, device):
        start = (device * NEAR_DEV).astype(jnp.int32)
        tiles = lax.dynamic_slice_in_dim(near_tiles, start, NEAR_DEV, 0).astype(jnp.float32)
        targets = lax.dynamic_slice_in_dim(near_tgt, start, NEAR_DEV, 0)
        sources = lax.dynamic_slice_in_dim(near_src, start, NEAR_DEV, 0)
        picked = leaf_charges[(device * SRC_TILES_DEV + sources).astype(jnp.int32)]
        products = jnp.einsum('kab,kbn->kan', tiles, picked, precision=lax.Precision.HIGHEST)
        rounded = lax.optimization_barrier(products.astype(jnp.bfloat16)).astype(jnp.float32)
        rows = (dest_block * TGT_TILES_DEV + targets).astype(jnp.int32)
        return accum.at[rows].add(rounded), None

    start_acc = jnp.zeros((TGT_TILES, TILE, NRHS), jnp.float32)
    devices_idx = jnp.arange(N_SRC * N_TGT).astype(jnp.int32)
    accum, _ = lax.scan(near_step, start_acc, devices_idx)

    blocks = leaf_charges.reshape(N_SRC, N_TGT, SRC_TILES_DEV, TILE, NRHS)
    bases = leaf_basis.astype(jnp.float32).reshape(N_SRC, N_TGT, SRC_TILES_DEV, RANK, TILE)
    roots = jnp.einsum('stirp,stipn->strn', bases, blocks, precision=lax.Precision.HIGHEST)
    table = jax.vmap(climb)(transfer, roots)
    table_b = lax.optimization_barrier(table.astype(jnp.bfloat16))
    target_f = target_basis.astype(jnp.float32)

    def far_step(total, block):
        nodes = far_node[block]
        picked = table_b[block][nodes].astype(jnp.float32)
        stacked = picked.reshape(TGT_TILES, FAR_PER * RANK, NRHS)
        mats = coupling[block].astype(jnp.float32)
        zed = jnp.einsum('trc,tcn->trn', mats, stacked, precision=lax.Precision.HIGHEST)
        zed_b = lax.optimization_barrier(zed.astype(jnp.bfloat16)).astype(jnp.float32)
        return total + jnp.einsum('trp,trn->tpn', target_f, zed_b, precision=lax.Precision.HIGHEST), None

    accum, _ = lax.scan(far_step, accum, jnp.arange(N_SRC).astype(jnp.int32))
    return accum.reshape(TGT_TILES * TILE, NRHS).astype(jnp.bfloat16)
```

```python
import functools

import jax
import jax.numpy as jnp
from jax import lax
from jax.experimental import pallas as pl
from jax.experimental.pallas import tpu as pltpu
from jax.sharding import PartitionSpec as P

CHUNKS = 1
F32, BF16 = jnp.float32, jnp.bfloat16
NT = (((1,), (1,)), ((), ()))
SMEM = pl.BlockSpec(memory_space=pltpu.SMEM)
VMEM = pl.BlockSpec(memory_space=pltpu.VMEM)
PARAMS = pltpu.CompilerParams(vmem_limit_bytes=48 * 2**20)


def tree_width(rank):
    return 2 * rank


def root_kernel(x_ref, basis_ref, tgt_ref, out_ref):
    leaves, rank, tile = basis_ref.shape
    nrhs = x_ref.shape[0]
    acc = jnp.zeros((nrhs, rank), F32)
    for i in range(leaves):
        acc += lax.dot_general(
            x_ref[:, i * tile : (i + 1) * tile], basis_ref[i], NT, preferred_element_type=F32
        )
    out_ref[:nrhs, :rank] = acc
    out_ref[nrhs:, :] = jnp.broadcast_to(tgt_ref[...].astype(F32), (8, out_ref.shape[1]))


def near_kernel(block_ref, src_ref, x_ref, tiles_ref, *out_refs):
    slots, tile, _ = tiles_ref.shape
    rows = out_refs[0].shape[0]
    first = block_ref[0] * slots
    for k in range(slots):
        leaf = src_ref[first + k]
        x = x_ref[:, pl.ds(pl.multiple_of(leaf * tile, tile), tile)]
        y = lax.dot_general(x, tiles_ref[k], NT, preferred_element_type=F32).astype(BF16)
        for c, out_ref in enumerate(out_refs):
            out_ref[:, k * tile : (k + 1) * tile] = y[c * rows : (c + 1) * rows]


def near_products(block, near_src, x, tiles, groups):
    slots = tiles.shape[0] // groups
    tile = tiles.shape[1]
    nrhs, width = x.shape
    rows = nrhs // CHUNKS
    return pl.pallas_call(
        near_kernel,
        out_shape=[jax.ShapeDtypeStruct((rows, slots * tile), BF16)] * CHUNKS,
        grid_spec=pltpu.PrefetchScalarGridSpec(
            num_scalar_prefetch=2,
            grid=(1,),
            in_specs=[
                pl.BlockSpec((nrhs, width), lambda i, b, s: (0, 0)),
                pl.BlockSpec((slots, tile, tile), lambda i, b, s: (b[0], 0, 0)),
            ],
            out_specs=[pl.BlockSpec((rows, slots * tile), lambda i, b, s: (0, 0))] * CHUNKS,
        ),
        compiler_params=PARAMS,
    )(block, near_src, x, tiles)


def far_kernel(groups, me_ref, node_ref, *refs):
    root_refs = refs[:groups]
    edge_ref, coupling_ref, basis_ref, out_ref, exact, low, high = refs[groups:]
    step = pl.program_id(0)
    leaves, rank, tile = basis_ref.shape
    per = coupling_ref.shape[2] // rank
    chunks, rows = out_ref.shape[0], out_ref.shape[2]
    nrhs = chunks * rows

    @pl.when(step == 0)
    def _():
        for m in range(groups):
            exact[groups - 1 + (me_ref[0] ^ m)] = root_refs[m][:nrhs, :rank]
        for n in range(groups - 2, -1, -1):
            pair = jnp.concatenate([exact[2 * n + 1], exact[2 * n + 2]], axis=1)
            exact[n] = lax.dot_general(
                pair, edge_ref[n], NT, precision=lax.Precision.HIGHEST, preferred_element_type=F32
            )
        zero = jnp.zeros((nrhs, rank), BF16)
        for n in range(2 * groups - 1):
            node = exact[n].astype(BF16)
            low[n] = jnp.concatenate([node, zero], axis=1)
            high[n] = jnp.concatenate([zero, node], axis=1)

    for i in range(leaves):
        tau = step * leaves + i
        nodes = [node_ref[tau * per + k] for k in range(per)]
        stacked = jnp.concatenate(
            [low[nodes[k]] + high[nodes[k + 1]] for k in range(0, per, 2)], axis=1
        )
        z = lax.dot_general(stacked, coupling_ref[i], NT, preferred_element_type=F32).astype(BF16)
        far = jnp.dot(z, basis_ref[i], preferred_element_type=F32)
        for c in range(chunks):
            out_ref[c, 0, :, i * tile : (i + 1) * tile] = far[c * rows : (c + 1) * rows]


def far_field(me, far_node, roots, transfer, coupling, target_basis, pieces):
    groups = len(roots)
    tgt_tiles, rank, tile = target_basis.shape
    leaves = tgt_tiles // pieces
    nrhs = roots[0].shape[0] - 8
    rows = nrhs // CHUNKS
    nodes = 2 * groups - 1
    return pl.pallas_call(
        functools.partial(far_kernel, groups),
        out_shape=jax.ShapeDtypeStruct((CHUNKS, pieces, rows, leaves * tile), F32),
        grid_spec=pltpu.PrefetchScalarGridSpec(
            num_scalar_prefetch=2,
            grid=(pieces,),
            in_specs=[pl.BlockSpec(r.shape, lambda i, a, b: (0, 0)) for r in roots]
            + [
                pl.BlockSpec(transfer.shape, lambda i, a, b: (0, 0, 0)),
                pl.BlockSpec((leaves,) + coupling.shape[1:], lambda i, a, b: (i, 0, 0)),
                pl.BlockSpec((leaves, rank, tile), lambda i, a, b: (i, 0, 0)),
            ],
            out_specs=pl.BlockSpec((CHUNKS, 1, rows, leaves * tile), lambda i, a, b: (0, i, 0, 0)),
            scratch_shapes=[
                pltpu.VMEM((nodes, nrhs, rank), F32),
                pltpu.VMEM((nodes, nrhs, 2 * rank), BF16),
                pltpu.VMEM((nodes, nrhs, 2 * rank), BF16),
            ],
        ),
        compiler_params=PARAMS,
    )(me, far_node, *roots, transfer, coupling, target_basis)


def gather_kernel(chunk, groups, core_ref, tgt_ref, far_ref, *refs):
    got_refs = refs[:groups]
    keep_ref, send_ref, acc = refs[groups:]
    pieces, rows, width = acc.shape
    slots = tgt_ref.shape[0] // groups
    tile = got_refs[0].shape[1] // slots
    leaves = width // tile
    acc[...] = far_ref[0]
    for m in range(groups):
        for k in range(slots):
            leaf = tgt_ref[m * slots + k]
            piece = leaf // leaves
            spot = pl.ds(pl.multiple_of((leaf - piece * leaves) * tile, tile), tile)
            acc[piece, :, spot] = acc[piece, :, spot] + got_refs[m][
                :, k * tile : (k + 1) * tile
            ].astype(F32)
    core = core_ref[0]
    for z in range(pieces // 2):
        keep_ref[z] = acc[2 * z + core]
        send_ref[z] = acc[2 * z + 1 - core].astype(BF16)


def gather_near(chunk, core, tgt, far, got):
    _, pieces, rows, width = far.shape
    groups = len(got)
    half = (pieces // 2, rows, width)
    return pl.pallas_call(
        functools.partial(gather_kernel, chunk, groups),
        out_shape=[jax.ShapeDtypeStruct(half, F32), jax.ShapeDtypeStruct(half, BF16)],
        grid_spec=pltpu.PrefetchScalarGridSpec(
            num_scalar_prefetch=2,
            grid=(1,),
            in_specs=[pl.BlockSpec((1, pieces, rows, width), lambda i, a, b: (chunk, 0, 0, 0))]
            + [pl.BlockSpec(g.shape, lambda i, a, b: (0, 0)) for g in got],
            out_specs=[pl.BlockSpec(half, lambda i, a, b: (0, 0, 0))] * 2,
            scratch_shapes=[pltpu.VMEM((pieces, rows, width), F32)],
        ),
        compiler_params=PARAMS,
    )(core, tgt, far, *got)


def place_kernel(count, me_ref, *refs):
    piece_refs, out_ref, sems = refs[:count], refs[count], refs[count + 1]
    pieces = count // CHUNKS
    rows, width = piece_refs[0].shape
    copies = []
    for c in range(CHUNKS):
        for m in range(pieces):
            owner = me_ref[0] ^ m
            spot = pl.ds(pl.multiple_of(owner * width, width), width)
            n = c * pieces + m
            copies.append(
                pltpu.make_async_copy(
                    piece_refs[n], out_ref.at[pl.ds(c * rows, rows), spot], sems.at[n]
                )
            )
    for copy in copies:
        copy.start()
    for copy in copies:
        copy.wait()


def place(me, parts):
    rows, width = parts[0].shape
    pieces = len(parts) // CHUNKS
    return pl.pallas_call(
        functools.partial(place_kernel, len(parts)),
        out_shape=jax.ShapeDtypeStruct((rows * CHUNKS, width * pieces), BF16),
        in_specs=[SMEM] + [pl.BlockSpec(memory_space=pl.ANY)] * len(parts),
        out_specs=pl.BlockSpec(memory_space=pl.ANY),
        scratch_shapes=[pltpu.SemaphoreType.DMA((len(parts),))],
    )(me, *parts)


def swap(value, axis, mask):
    size = lax.axis_size(axis)
    return lax.ppermute(value, axis, [(i, i ^ mask) for i in range(size)])


def shards(
    charges, near_tiles, near_tgt, near_src, leaf_basis, transfer, coupling, far_node, target_basis
):
    groups = lax.axis_size("tgt")
    sources = lax.axis_size("src")
    me_t = lax.axis_index("tgt").astype(jnp.int32)
    me_s = lax.axis_index("src").astype(jnp.int32)
    core, me_z = me_s % 2, me_s // 2
    tiles, tile, _ = near_tiles.shape
    slots = tiles // groups
    nrhs = charges.shape[1]
    x = charges.T

    message = pl.pallas_call(
        root_kernel,
        out_shape=jax.ShapeDtypeStruct((nrhs + 8, tiles), F32),
        in_specs=[VMEM] * 3,
        out_specs=VMEM,
        compiler_params=PARAMS,
    )(x, leaf_basis, near_tgt.reshape(1, tiles))
    messages = [message] + [swap(message, "tgt", m) for m in range(1, groups)]

    products = [
        near_products((me_t ^ m).reshape(1), near_src, x, near_tiles, groups)
        for m in range(groups)
    ]
    targets = jnp.concatenate(
        [
            lax.dynamic_slice(msg, (nrhs, me_t * slots), (1, slots))[0].astype(jnp.int32)
            for msg in messages
        ]
    )
    far = far_field(
        me_t.reshape(1),
        far_node[0].reshape(-1),
        messages,
        transfer[0],
        coupling[0],
        target_basis,
        sources,
    )
    parts = []
    for c in range(CHUNKS):
        got = [products[0][c]] + [swap(products[m][c], "tgt", m) for m in range(1, groups)]
        keep, send = gather_near(c, core.reshape(1), targets, far, got)
        total = keep + swap(send, "src", 1).astype(F32)
        final = total[me_z]
        for m in range(1, sources // 2):
            final = final + swap(total[me_z ^ m].astype(BF16), "src", 2 * m).astype(F32)
        final = final.astype(BF16)
        mine = [final] + [swap(final, "src", 2 * m) for m in range(1, sources // 2)]
        other = [swap(p, "src", 1) for p in mine]
        for a, b in zip(mine, other):
            parts += [a, b]
    return place(me_s.reshape(1), parts).T


def solution(mesh):
    in_specs = (
        P(("src", "tgt"), None),
        P(("src", "tgt"), None, None),
        P(("src", "tgt")),
        P(("src", "tgt")),
        P(("src", "tgt"), None, None),
        P("src", None, None, None),
        P("src", "tgt", None, None),
        P("src", "tgt", None),
        P("tgt", None, None),
    )
    out_specs = P("tgt", None)
    return jax.shard_map(shards, mesh=mesh, in_specs=in_specs, out_specs=out_specs, check_vma=False)
```

```python
import functools

import jax
import jax.numpy as jnp
from jax import lax
from jax.experimental import pallas as pl
from jax.experimental.pallas import tpu as pltpu
from jax.sharding import PartitionSpec as P

NEAR_SPLIT = 4
FAR_STEPS = 4
F32, BF16 = jnp.float32, jnp.bfloat16
NT = (((1,), (1,)), ((), ()))
SMEM = pl.BlockSpec(memory_space=pltpu.SMEM)
VMEM = pl.BlockSpec(memory_space=pltpu.VMEM)
ANY = pl.BlockSpec(memory_space=pl.ANY)


def root_kernel(x_ref, basis_ref, tgt_ref, out_ref):
    leaves, rank, tile = basis_ref.shape
    nrhs = x_ref.shape[0]
    acc = jnp.zeros((nrhs, rank), F32)
    for i in range(leaves):
        acc += lax.dot_general(
            x_ref[:, i * tile : (i + 1) * tile], basis_ref[i], NT, preferred_element_type=F32
        )
    out_ref[:nrhs, :rank] = acc
    out_ref[nrhs:, :] = jnp.broadcast_to(tgt_ref[...].astype(F32), (8, out_ref.shape[1]))


def near_kernel(masks, groups, me_ref, src_ref, x_ref, tiles_ref, *refs):
    out_refs, held, sems = refs[:-2], refs[-2], refs[-1]
    tile = held.shape[1]
    slots = held.shape[0] // len(masks)
    step = slots // NEAR_SPLIT
    firsts = [(me_ref[0] ^ m) * slots for m in masks]
    copies = [
        pltpu.make_async_copy(
            tiles_ref.at[pl.ds(first + j * step, step)],
            held.at[pl.ds(n * slots + j * step, step)],
            sems.at[n * NEAR_SPLIT + j],
        )
        for n, first in enumerate(firsts)
        for j in range(NEAR_SPLIT)
    ]
    for copy in copies:
        copy.start()
    for n, first in enumerate(firsts):
        for k in range(slots):
            if k % step == 0:
                copies[n * NEAR_SPLIT + k // step].wait()
            leaf = src_ref[first + k]
            x = x_ref[:, pl.ds(pl.multiple_of(leaf * tile, tile), tile)]
            y = lax.dot_general(x, held[n * slots + k], NT, preferred_element_type=F32)
            out_refs[n][:, k * tile : (k + 1) * tile] = y.astype(BF16)


def near_products(masks, me, near_src, x, tiles, groups):
    count, tile, _ = tiles.shape
    slots = count // groups
    nrhs = x.shape[0]
    return pl.pallas_call(
        functools.partial(near_kernel, masks, groups),
        out_shape=[jax.ShapeDtypeStruct((nrhs, slots * tile), BF16)] * len(masks),
        in_specs=[SMEM, SMEM, VMEM, ANY],
        out_specs=[VMEM] * len(masks),
        scratch_shapes=[
            pltpu.VMEM((slots * len(masks), tile, tile), BF16),
            pltpu.SemaphoreType.DMA((NEAR_SPLIT * len(masks),)),
        ],
        compiler_params=pltpu.CompilerParams(vmem_limit_bytes=58 * 2**20),
        cost_estimate=pl.CostEstimate(
            flops=2 * slots * len(masks) * tile * tile * nrhs,
            bytes_accessed=slots * len(masks) * tile * (tile + nrhs) * 2,
            transcendentals=0,
        ),
    )(me, near_src, x, tiles)


def far_kernel(groups, me_ref, node_ref, *refs):
    root_refs = refs[:groups]
    edge_ref, coupling_ref, basis_ref, out_ref, exact, low, high = refs[groups:]
    step = pl.program_id(0)
    leaves, rank, tile = basis_ref.shape
    per = coupling_ref.shape[2] // rank
    nrhs = out_ref.shape[1]

    @pl.when(step == 0)
    def _():
        for m in range(groups):
            exact[groups - 1 + (me_ref[0] ^ m)] = root_refs[m][:nrhs, :rank]
        for n in range(groups - 2, -1, -1):
            pair = jnp.concatenate([exact[2 * n + 1], exact[2 * n + 2]], axis=1)
            exact[n] = lax.dot_general(
                pair, edge_ref[n], NT, precision=lax.Precision.HIGHEST, preferred_element_type=F32
            )
        zero = jnp.zeros((nrhs, rank), BF16)
        for n in range(2 * groups - 1):
            node = exact[n].astype(BF16)
            low[n] = jnp.concatenate([node, zero], axis=1)
            high[n] = jnp.concatenate([zero, node], axis=1)

    zs = []
    for i in range(leaves):
        tau = step * leaves + i
        nodes = [node_ref[tau * per + k] for k in range(per)]
        stacked = jnp.concatenate(
            [low[nodes[k]] + high[nodes[k + 1]] for k in range(0, per, 2)], axis=1
        )
        zs.append(
            lax.dot_general(stacked, coupling_ref[i], NT, preferred_element_type=F32).astype(BF16)
        )
    wide = out_ref.shape[2] // tile
    for i in range(leaves):
        at = (i % wide) * tile
        out_ref[i // wide, :, at : at + tile] = jnp.dot(
            zs[i], basis_ref[i], preferred_element_type=F32
        )


def far_field(me, far_node, roots, transfer, coupling, target_basis, pieces):
    groups = len(roots)
    tgt_tiles, rank, tile = target_basis.shape
    leaves = tgt_tiles // FAR_STEPS
    nrhs = roots[0].shape[0] - 8
    nodes = 2 * groups - 1
    many = pieces // FAR_STEPS
    width = tgt_tiles // pieces * tile
    return pl.pallas_call(
        functools.partial(far_kernel, groups),
        out_shape=jax.ShapeDtypeStruct((pieces, nrhs, width), F32),
        grid_spec=pltpu.PrefetchScalarGridSpec(
            num_scalar_prefetch=2,
            grid=(FAR_STEPS,),
            in_specs=[pl.BlockSpec(r.shape, lambda i, a, b: (0, 0)) for r in roots]
            + [
                pl.BlockSpec(transfer.shape, lambda i, a, b: (0, 0, 0)),
                pl.BlockSpec((leaves,) + coupling.shape[1:], lambda i, a, b: (i, 0, 0)),
                pl.BlockSpec((leaves, rank, tile), lambda i, a, b: (i, 0, 0)),
            ],
            out_specs=pl.BlockSpec((many, nrhs, width), lambda i, a, b: (i, 0, 0)),
            scratch_shapes=[
                pltpu.VMEM((nodes, nrhs, rank), F32),
                pltpu.VMEM((nodes, nrhs, 2 * rank), BF16),
                pltpu.VMEM((nodes, nrhs, 2 * rank), BF16),
            ],
        ),
        compiler_params=pltpu.CompilerParams(vmem_limit_bytes=24 * 2**20),
        cost_estimate=pl.CostEstimate(
            flops=2 * tgt_tiles * nrhs * (coupling.shape[1] * coupling.shape[2] + rank * tile),
            bytes_accessed=(coupling.size + target_basis.size) * 2 + tgt_tiles * tile * nrhs * 4,
            transcendentals=0,
        ),
    )(me, far_node, *roots, transfer, coupling, target_basis)


def gather_kernel(groups, core_ref, tgt_ref, far_ref, *refs):
    got_refs, (acc, send_ref) = refs[:groups], refs[groups:]
    pieces, rows, width = acc.shape
    slots = tgt_ref.shape[0] // groups
    tile = got_refs[0].shape[1] // slots
    leaves = width // tile
    for m in range(groups):
        for k in range(slots):
            leaf = tgt_ref[m * slots + k]
            piece = leaf // leaves
            spot = pl.ds(pl.multiple_of((leaf - piece * leaves) * tile, tile), tile)
            acc[piece, :, spot] = acc[piece, :, spot] + got_refs[m][
                :, k * tile : (k + 1) * tile
            ].astype(F32)
    core = core_ref[0]
    for z in range(pieces // 2):
        send_ref[z] = acc[2 * z + 1 - core].astype(BF16)


def gather_near(core, tgt, far, got):
    pieces, rows, width = far.shape
    groups = len(got)
    return pl.pallas_call(
        functools.partial(gather_kernel, groups),
        out_shape=[
            jax.ShapeDtypeStruct(far.shape, F32),
            jax.ShapeDtypeStruct((pieces // 2, rows, width), BF16),
        ],
        in_specs=[SMEM, SMEM, VMEM] + [VMEM] * groups,
        out_specs=[VMEM, VMEM],
        input_output_aliases={2: 0},
        compiler_params=pltpu.CompilerParams(vmem_limit_bytes=16 * 2**20),
    )(core, tgt, far, *got)


def split_kernel(masks, me_ref, acc_ref, got_ref, *out_refs):
    z, core = me_ref[0] // 2, me_ref[0] % 2
    for m, out_ref in zip(masks, out_refs):
        piece = z ^ m
        out_ref[...] = (acc_ref[2 * piece + core] + got_ref[piece].astype(F32)).astype(
            out_ref.dtype
        )


def split(masks, dtypes, me, acc, got):
    return pl.pallas_call(
        functools.partial(split_kernel, masks),
        out_shape=[jax.ShapeDtypeStruct(got.shape[1:], d) for d in dtypes],
        in_specs=[SMEM, VMEM, VMEM],
        out_specs=[VMEM] * len(masks),
        compiler_params=pltpu.CompilerParams(vmem_limit_bytes=16 * 2**20),
    )(me, acc, got)


def place_kernel(masks, me_ref, *refs):
    out_ref = refs[-1]
    for m, piece_ref in zip(masks, refs):
        width = piece_ref.shape[1]
        spot = pl.ds(pl.multiple_of((me_ref[0] ^ m) * width, width), width)
        out_ref[:, spot] = piece_ref[...]


def place(masks, me, parts):
    rows, width = parts[0].shape
    return pl.pallas_call(
        functools.partial(place_kernel, masks),
        out_shape=jax.ShapeDtypeStruct((rows, width * len(parts)), BF16),
        in_specs=[SMEM] + [VMEM] * len(parts),
        out_specs=VMEM,
        compiler_params=pltpu.CompilerParams(vmem_limit_bytes=16 * 2**20),
    )(me, *parts)


def swap(value, axis, mask):
    size = lax.axis_size(axis)
    return lax.ppermute(value, axis, [(i, i ^ mask) for i in range(size)])


def tied(value, *others):
    return lax.optimization_barrier((value,) + others)[0]


def sum_and_share(me, acc, got):
    chips = acc.shape[0] // 2
    if chips == 4:
        masks = (3, 2, 1, 0)
        first, cross, near, own = split(masks, (BF16, F32, BF16, F32), me, acc, got)
        a = swap(first, "src", 2)
        cross = (cross + a.astype(F32)).astype(BF16)
        b = swap(cross, "src", 4)
        c = swap(tied(near, cross), "src", 2)
        own = (own + b.astype(F32) + c.astype(F32)).astype(BF16)
        d = swap(own, "src", 4)
        e = swap(own, "src", 2)
        return (0, 1, 2, 3), [own, e, d, swap(d, "src", 2)]
    masks = tuple(range(chips))
    dtypes = (F32,) + (BF16,) * (chips - 1)
    own, *rest = split(masks, dtypes, me, acc, got)
    for m, part in zip(masks[1:], rest):
        own = own + swap(part, "src", 2 * m).astype(F32)
    own = own.astype(BF16)
    return masks, [own] + [swap(own, "src", 2 * m) for m in masks[1:]]


def shards(
    charges, near_tiles, near_tgt, near_src, leaf_basis, transfer, coupling, far_node, target_basis
):
    groups = lax.axis_size("tgt")
    sources = lax.axis_size("src")
    me_t = lax.axis_index("tgt").astype(jnp.int32)
    me_s = lax.axis_index("src").astype(jnp.int32)
    tiles, tile, _ = near_tiles.shape
    slots = tiles // groups
    nrhs = charges.shape[1]
    x = charges.T
    me = me_t.reshape(1)

    masks = sorted(range(groups), key=lambda m: -bin(m).count("1"))
    (first,) = near_products(masks[:1], me, near_src, x, near_tiles, groups)
    x_late = tied(x, first)
    message = pl.pallas_call(
        root_kernel,
        out_shape=jax.ShapeDtypeStruct((nrhs + 8, tiles), F32),
        in_specs=[VMEM] * 3,
        out_specs=VMEM,
        compiler_params=pltpu.CompilerParams(vmem_limit_bytes=16 * 2**20),
    )(x_late, leaf_basis, near_tgt.reshape(1, tiles))
    messages = [message] + [swap(message, "tgt", m) for m in range(1, groups)]
    rest = near_products(masks[1:], me, near_src, x_late, near_tiles, groups)
    got = [swap(y, "tgt", m) if m else y for m, y in zip(masks, [first, *rest])]
    far = far_field(
        me,
        far_node[0].reshape(-1),
        messages,
        transfer[0],
        coupling[0],
        target_basis,
        sources,
    )
    targets = jnp.concatenate(
        [
            lax.dynamic_slice(messages[m], (nrhs, me_t * slots), (1, slots))[0].astype(jnp.int32)
            for m in masks
        ]
    )
    acc, send = gather_near((me_s % 2).reshape(1), targets, far, got)
    owners, mine = sum_and_share(me_s.reshape(1), acc, swap(send, "src", 1))
    other = [swap(p, "src", 1) for p in mine]
    spots = [2 * m for m in owners] + [2 * m + 1 for m in owners]
    return place(spots, me_s.reshape(1), mine + other).T


def solution(mesh):
    in_specs = (
        P(("src", "tgt"), None),
        P(("src", "tgt"), None, None),
        P(("src", "tgt")),
        P(("src", "tgt")),
        P(("src", "tgt"), None, None),
        P("src", None, None, None),
        P("src", "tgt", None, None),
        P("src", "tgt", None),
        P("tgt", None, None),
    )
    out_specs = P("tgt", None)
    return jax.shard_map(shards, mesh=mesh, in_specs=in_specs, out_specs=out_specs, check_vma=False)
```

```python
import functools
import typing

import jax
import jax.numpy as jnp
from jax import lax
from jax.experimental import pallas as pl
from jax.experimental.pallas import tpu as pltpu
from jax.sharding import PartitionSpec as P

STEP = 8
HEAD = 8
FIRST_HEAD = 32
FAR_PIECES = 2
NEAR_VMEM = 60
F32, BF16 = jnp.float32, jnp.bfloat16
NT = (((1,), (1,)), ((), ()))
SMEM = pl.BlockSpec(memory_space=pltpu.SMEM)
LONG = pl.CostEstimate(flops=2**36, bytes_accessed=2**24, transcendentals=0)
VMEM = pl.BlockSpec(memory_space=pltpu.VMEM)
ANY = pl.BlockSpec(memory_space=pl.ANY)


class Part(typing.NamedTuple):
    mask: int
    slots: int
    begin: int
    end: int
    head: bool


def near_kernel(parts, me_ref, src_ref, tgt_ref, x_hbm, basis_ref, tiles_ref, *refs):
    outs, (x_ref, basis, held, sems) = refs[: len(parts)], refs[len(parts) :]
    tile = held.shape[1]
    leaves, rank, _ = basis.shape
    nrhs = x_ref.shape[0]
    count = tiles_ref.shape[0]
    slots = parts[0].slots
    extra = [
        pltpu.make_async_copy(x_hbm, x_ref, sems.at[0]),
        pltpu.make_async_copy(basis_ref, basis, sems.at[1]),
    ]
    copies, spans, at = [], [], 0
    for part in parts:
        first = (me_ref[0] ^ part.mask) * slots
        for k in range(part.begin, part.end, STEP):
            size = min(STEP, part.end - k)
            spans.append((part, k, size, at))
            copies.append(
                pltpu.make_async_copy(
                    tiles_ref.at[pl.ds(first + k, size)],
                    held.at[pl.ds(at, size)],
                    sems.at[2 + len(copies)],
                )
            )
            at += size
    for copy in extra + copies:
        copy.start()
    for copy in extra:
        copy.wait()
    if any(part.head for part in parts):
        root = jnp.zeros((nrhs, rank), F32)
        for i in range(leaves):
            root += lax.dot_general(
                x_ref[:, i * tile : (i + 1) * tile], basis[i], NT, preferred_element_type=F32
            )
        high = root.astype(BF16)
        low = (root - high.astype(F32)).astype(BF16)
        roots = jnp.concatenate([high, low], axis=1)
        tgt = jnp.broadcast_to(tgt_ref[...].astype(F32).astype(BF16), (nrhs, count))
        for part, out in zip(parts, outs):
            if part.head:
                end = out.shape[1] - count
                out[:, end - 2 * rank : end] = roots
                out[:, end:] = tgt
    for (part, begin, size, at), copy in zip(spans, copies):
        copy.wait()
        first = (me_ref[0] ^ part.mask) * slots
        out = outs[parts.index(part)]
        for k in range(size):
            leaf = src_ref[first + begin + k]
            x = x_ref[:, pl.ds(pl.multiple_of(leaf * tile, tile), tile)]
            y = lax.dot_general(x, held[at + k], NT, preferred_element_type=F32)
            spot = (begin - part.begin + k) * tile
            out[:, spot : spot + tile] = y.astype(BF16)


def near_products(parts, me, near_src, near_tgt, x, basis, tiles):
    count, tile, _ = tiles.shape
    nrhs, rank = x.shape[0], basis.shape[1]
    widths = [(p.end - p.begin) * tile + (2 * rank + count if p.head else 0) for p in parts]
    blocks = sum(-(-(p.end - p.begin) // STEP) for p in parts)
    return pl.pallas_call(
        functools.partial(near_kernel, parts),
        out_shape=[jax.ShapeDtypeStruct((nrhs, w), BF16) for w in widths],
        in_specs=[SMEM, SMEM, VMEM, ANY, ANY, ANY],
        out_specs=[VMEM] * len(widths),
        scratch_shapes=[
            pltpu.VMEM(x.shape, BF16),
            pltpu.VMEM(basis.shape, BF16),
            pltpu.VMEM((sum(p.end - p.begin for p in parts), tile, tile), BF16),
            pltpu.SemaphoreType.DMA((blocks + 2,)),
        ],
        compiler_params=pltpu.CompilerParams(vmem_limit_bytes=NEAR_VMEM * 2**20),
    )(me, near_src, near_tgt.reshape(1, count), x, basis, tiles)


def add_products(acc, tgt_ref, me, parts, got_refs, tile):
    leaves = acc.shape[2] // tile
    for n, (part, got_ref) in enumerate(zip(parts, got_refs)):
        for k in range(part.begin, part.end):
            leaf = tgt_ref[n, me * part.slots + k]
            piece = leaf // leaves
            spot = pl.ds(pl.multiple_of((leaf - piece * leaves) * tile, tile), tile)
            at = (k - part.begin) * tile
            got = got_ref[:, at : at + tile].astype(F32)
            acc[piece, :, spot] = acc[piece, :, spot] + got


def start_kernel(parts, tile, me_ref, tgt_ref, *refs):
    acc = refs[-1]
    acc[...] = jnp.zeros_like(acc)
    add_products(acc, tgt_ref, me_ref[0], parts, refs[:-1], tile)


def start_near(parts, me, tgt, got, pieces, width, tile):
    return pl.pallas_call(
        functools.partial(start_kernel, parts, tile),
        out_shape=jax.ShapeDtypeStruct((pieces, got[0].shape[0], width), F32),
        in_specs=[SMEM, SMEM] + [VMEM] * len(got),
        out_specs=VMEM,
        cost_estimate=LONG,
        compiler_params=pltpu.CompilerParams(vmem_limit_bytes=16 * 2**20),
    )(me, tgt, *got)


def far_kernel(groups, count, me_ref, node_ref, *refs):
    head_refs = refs[:groups]
    edge_ref, coupling_ref, basis_ref, near_ref, out_ref, exact, low, high = refs[groups:]
    tgt_tiles, rank, tile = basis_ref.shape
    per = coupling_ref.shape[2] // rank
    pieces, nrhs, width = out_ref.shape
    leaves = width // tile
    for m in range(groups):
        end = head_refs[m].shape[1] - count
        pair = head_refs[m][:, end - 2 * rank : end].astype(F32)
        exact[groups - 1 + (me_ref[0] ^ m)] = pair[:, :rank] + pair[:, rank:]
    for n in range(groups - 2, -1, -1):
        pair = jnp.concatenate([exact[2 * n + 1], exact[2 * n + 2]], axis=1)
        exact[n] = lax.dot_general(
            pair, edge_ref[n], NT, precision=lax.Precision.HIGHEST, preferred_element_type=F32
        )
    zero = jnp.zeros((nrhs, rank), BF16)
    for n in range(2 * groups - 1):
        node = exact[n].astype(BF16)
        low[n] = jnp.concatenate([node, zero], axis=1)
        high[n] = jnp.concatenate([zero, node], axis=1)

    @pl.loop(0, pieces // FAR_PIECES)
    def _(block):
        first = block * FAR_PIECES
        zs = []
        for i in range(FAR_PIECES * leaves):
            tau = first * leaves + i
            nodes = [node_ref[tau * per + k] for k in range(per)]
            stacked = jnp.concatenate(
                [low[nodes[k]] + high[nodes[k + 1]] for k in range(0, per, 2)], axis=1
            )
            z = lax.dot_general(stacked, coupling_ref[tau], NT, preferred_element_type=F32)
            zs.append(z.astype(BF16))
        for i in range(FAR_PIECES * leaves):
            far = jnp.dot(zs[i], basis_ref[first * leaves + i], preferred_element_type=F32)
            p, at = first + i // leaves, slice(i % leaves * tile, (i % leaves + 1) * tile)
            out_ref[p, :, at] = near_ref[p, :, at] + far


def far_field(me, far_node, heads, transfer, coupling, target_basis, near, count):
    groups = len(heads)
    rank = target_basis.shape[1]
    nrhs = near.shape[1]
    nodes = 2 * groups - 1
    return pl.pallas_call(
        functools.partial(far_kernel, groups, count),
        out_shape=jax.ShapeDtypeStruct(near.shape, F32),
        in_specs=[SMEM, SMEM] + [VMEM] * (groups + 4),
        out_specs=VMEM,
        scratch_shapes=[
            pltpu.VMEM((nodes, nrhs, rank), F32),
            pltpu.VMEM((nodes, nrhs, 2 * rank), BF16),
            pltpu.VMEM((nodes, nrhs, 2 * rank), BF16),
        ],
        input_output_aliases={groups + 5: 0},
        compiler_params=pltpu.CompilerParams(vmem_limit_bytes=16 * 2**20),
    )(me, far_node, *heads, transfer, coupling, target_basis, near)


def gather_kernel(parts, tile, me_ref, core_ref, tgt_ref, far_ref, *refs):
    got_refs, (acc, send_ref) = refs[:-2], refs[-2:]
    add_products(acc, tgt_ref, me_ref[0], parts, got_refs, tile)
    for z in range(send_ref.shape[0]):
        send_ref[z] = acc[2 * z + 1 - core_ref[0]].astype(BF16)


def gather_near(parts, me, core, tgt, far, got, tile):
    pieces, rows, width = far.shape
    return pl.pallas_call(
        functools.partial(gather_kernel, parts, tile),
        out_shape=[
            jax.ShapeDtypeStruct(far.shape, F32),
            jax.ShapeDtypeStruct((pieces // 2, rows, width), BF16),
        ],
        in_specs=[SMEM] * 3 + [VMEM] * (1 + len(got)),
        out_specs=[VMEM, VMEM],
        input_output_aliases={3: 0},
        compiler_params=pltpu.CompilerParams(vmem_limit_bytes=16 * 2**20),
    )(me, core, tgt, far, *got)


def split_kernel(masks, me_ref, acc_ref, got_ref, *out_refs):
    z, core = me_ref[0] // 2, me_ref[0] % 2
    for m, out_ref in zip(masks, out_refs):
        piece = z ^ m
        out_ref[...] = (acc_ref[2 * piece + core] + got_ref[piece].astype(F32)).astype(
            out_ref.dtype
        )


def split(masks, dtypes, me, acc, got):
    return pl.pallas_call(
        functools.partial(split_kernel, masks),
        out_shape=[jax.ShapeDtypeStruct(got.shape[1:], d) for d in dtypes],
        in_specs=[SMEM, VMEM, VMEM],
        out_specs=[VMEM] * len(masks),
        compiler_params=pltpu.CompilerParams(vmem_limit_bytes=16 * 2**20),
    )(me, acc, got)


def place_kernel(masks, me_ref, *refs):
    out_ref = refs[-1]
    for m, piece_ref in zip(masks, refs):
        width = piece_ref.shape[1]
        spot = pl.ds(pl.multiple_of((me_ref[0] ^ m) * width, width), width)
        out_ref[:, spot] = piece_ref[...]


def place(masks, me, parts):
    rows, width = parts[0].shape
    return pl.pallas_call(
        functools.partial(place_kernel, masks),
        out_shape=jax.ShapeDtypeStruct((rows, width * len(parts)), BF16),
        in_specs=[SMEM] + [VMEM] * len(parts),
        out_specs=VMEM,
        compiler_params=pltpu.CompilerParams(vmem_limit_bytes=16 * 2**20),
    )(me, *parts)


def swap(value, axis, mask):
    size = lax.axis_size(axis)
    return lax.ppermute(value, axis, [(i, i ^ mask) for i in range(size)])


def tied(value, *others):
    return lax.optimization_barrier((value,) + others)[0]


def sum_and_share(me, acc, got):
    chips = acc.shape[0] // 2
    if chips == 4:
        masks = (3, 2, 1, 0)
        first, cross, near, own = split(masks, (BF16, F32, BF16, F32), me, acc, got)
        a = swap(first, "src", 2)
        cross = (cross + a.astype(F32)).astype(BF16)
        b = swap(cross, "src", 4)
        c = swap(tied(near, cross), "src", 2)
        own = (own + b.astype(F32) + c.astype(F32)).astype(BF16)
        d = swap(own, "src", 4)
        e = swap(own, "src", 2)
        return (0, 1, 2, 3), [own, e, d, swap(d, "src", 2)]
    masks = tuple(range(chips))
    dtypes = (F32,) + (BF16,) * (chips - 1)
    own, *rest = split(masks, dtypes, me, acc, got)
    for m, part in zip(masks[1:], rest):
        own = own + swap(part, "src", 2 * m).astype(F32)
    own = own.astype(BF16)
    return masks, [own] + [swap(own, "src", 2 * m) for m in masks[1:]]


def shards(
    charges, near_tiles, near_tgt, near_src, leaf_basis, transfer, coupling, far_node, target_basis
):
    groups = lax.axis_size("tgt")
    sources = lax.axis_size("src")
    me_t = lax.axis_index("tgt").astype(jnp.int32)
    me_s = lax.axis_index("src").astype(jnp.int32)
    count, tile, _ = near_tiles.shape
    slots = count // groups
    x = charges.T
    me, core = me_t.reshape(1), (me_s % 2).reshape(1)

    masks = sorted(range(groups), key=lambda m: -bin(m).count("1"))
    ends = [min(FIRST_HEAD, slots)] + [min(HEAD, slots)] * (groups - 2) + [slots]
    heads = [Part(m, slots, 0, e, True) for m, e in zip(masks, ends)]
    tails = [Part(m, slots, e, slots, False) for m, e in zip(masks, ends) if e < slots]
    first = near_products(heads[:1], me, near_src, near_tgt, x, leaf_basis, near_tiles)
    rest = near_products(
        heads[1:] + tails, me, near_src, near_tgt, tied(x, *first), leaf_basis, near_tiles
    )
    parts = heads + tails
    got = {
        part: swap(y, "tgt", part.mask) if part.mask else y
        for part, y in zip(parts, [*first, *rest])
    }
    by_mask = {part.mask: got[part] for part in heads}

    def targets(some):
        rows = [by_mask[part.mask][:1, -count:] for part in some]
        return jnp.concatenate(rows).astype(F32).astype(jnp.int32)

    early = [part for part in heads if part.mask in (masks[0], masks[-1])]
    late = [part for part in parts if part not in early]
    acc = start_near(
        early,
        me,
        targets(early),
        [got[part] for part in early],
        sources,
        target_basis.shape[0] // sources * tile,
        tile,
    )
    acc = far_field(
        me,
        far_node[0].reshape(-1),
        [by_mask[m] for m in range(groups)],
        transfer[0],
        coupling[0],
        target_basis,
        acc,
        count,
    )
    acc, send = gather_near(
        late, me, core, targets(late), acc, [got[part] for part in late], tile
    )
    owners, mine = sum_and_share(me_s.reshape(1), acc, swap(send, "src", 1))
    other = [swap(p, "src", 1) for p in mine]
    spots = [2 * m for m in owners] + [2 * m + 1 for m in owners]
    return place(spots, me_s.reshape(1), mine + other).T


def solution(mesh):
    in_specs = (
        P(("src", "tgt"), None),
        P(("src", "tgt"), None, None),
        P(("src", "tgt")),
        P(("src", "tgt")),
        P(("src", "tgt"), None, None),
        P("src", None, None, None),
        P("src", "tgt", None, None),
        P("src", "tgt", None),
        P("tgt", None, None),
    )
    out_specs = P("tgt", None)
    return jax.shard_map(shards, mesh=mesh, in_specs=in_specs, out_specs=out_specs, check_vma=False)
```

```python
import functools
import typing

import jax
import jax.numpy as jnp
from jax import lax
from jax.experimental import pallas as pl
from jax.experimental.pallas import tpu as pltpu
from jax.sharding import PartitionSpec as P

STEP = 8
HEAD = 8
FIRST_HEAD = 32
FAR_PIECES = 2
NEAR_VMEM = 60
F32, BF16 = jnp.float32, jnp.bfloat16
NT = (((1,), (1,)), ((), ()))
SMEM = pl.BlockSpec(memory_space=pltpu.SMEM)
LONG = pl.CostEstimate(flops=2**36, bytes_accessed=2**24, transcendentals=0)
VMEM = pl.BlockSpec(memory_space=pltpu.VMEM)
ANY = pl.BlockSpec(memory_space=pl.ANY)


class Part(typing.NamedTuple):
    mask: int
    slots: int
    begin: int
    end: int
    head: bool


def near_kernel(parts, me_ref, src_ref, tgt_ref, x_hbm, basis_ref, tiles_ref, *refs):
    outs, (x_ref, basis, held, sems) = refs[: len(parts)], refs[len(parts) :]
    tile = held.shape[1]
    leaves, rank, _ = basis.shape
    nrhs = x_ref.shape[0]
    count = tiles_ref.shape[0]
    slots = parts[0].slots
    extra = [
        pltpu.make_async_copy(x_hbm, x_ref, sems.at[0]),
        pltpu.make_async_copy(basis_ref, basis, sems.at[1]),
    ]
    copies, spans, at = [], [], 0
    for part in parts:
        first = (me_ref[0] ^ part.mask) * slots
        for k in range(part.begin, part.end, STEP):
            size = min(STEP, part.end - k)
            spans.append((part, k, size, at))
            copies.append(
                pltpu.make_async_copy(
                    tiles_ref.at[pl.ds(first + k, size)],
                    held.at[pl.ds(at, size)],
                    sems.at[2 + len(copies)],
                )
            )
            at += size
    for copy in extra + copies:
        copy.start()
    for copy in extra:
        copy.wait()
    if any(part.head for part in parts):
        root = jnp.zeros((nrhs, rank), F32)
        for i in range(leaves):
            root += lax.dot_general(
                x_ref[:, i * tile : (i + 1) * tile], basis[i], NT, preferred_element_type=F32
            )
        high = root.astype(BF16)
        low = (root - high.astype(F32)).astype(BF16)
        roots = jnp.concatenate([high, low], axis=1)
        tgt = jnp.broadcast_to(tgt_ref[...].astype(F32).astype(BF16), (nrhs, count))
        for part, out in zip(parts, outs):
            if part.head:
                end = out.shape[1] - count
                out[:, end - 2 * rank : end] = roots
                out[:, end:] = tgt
    for (part, begin, size, at), copy in zip(spans, copies):
        copy.wait()
        first = (me_ref[0] ^ part.mask) * slots
        out = outs[parts.index(part)]
        for k in range(size):
            leaf = src_ref[first + begin + k]
            x = x_ref[:, pl.ds(pl.multiple_of(leaf * tile, tile), tile)]
            y = lax.dot_general(x, held[at + k], NT, preferred_element_type=F32)
            spot = (begin - part.begin + k) * tile
            out[:, spot : spot + tile] = y.astype(BF16)


def near_products(parts, me, near_src, near_tgt, x, basis, tiles):
    count, tile, _ = tiles.shape
    nrhs, rank = x.shape[0], basis.shape[1]
    widths = [(p.end - p.begin) * tile + (2 * rank + count if p.head else 0) for p in parts]
    blocks = sum(-(-(p.end - p.begin) // STEP) for p in parts)
    return pl.pallas_call(
        functools.partial(near_kernel, parts),
        out_shape=[jax.ShapeDtypeStruct((nrhs, w), BF16) for w in widths],
        in_specs=[SMEM, SMEM, VMEM, ANY, ANY, ANY],
        out_specs=[VMEM] * len(widths),
        scratch_shapes=[
            pltpu.VMEM(x.shape, BF16),
            pltpu.VMEM(basis.shape, BF16),
            pltpu.VMEM((sum(p.end - p.begin for p in parts), tile, tile), BF16),
            pltpu.SemaphoreType.DMA((blocks + 2,)),
        ],
        compiler_params=pltpu.CompilerParams(vmem_limit_bytes=NEAR_VMEM * 2**20),
    )(me, near_src, near_tgt.reshape(1, count), x, basis, tiles)


def add_products(acc, tgt_ref, me, parts, got_refs, tile):
    leaves = acc.shape[2] // tile
    for n, (part, got_ref) in enumerate(zip(parts, got_refs)):
        for k in range(part.begin, part.end):
            leaf = tgt_ref[n, me * part.slots + k]
            piece = leaf // leaves
            spot = pl.ds(pl.multiple_of((leaf - piece * leaves) * tile, tile), tile)
            at = (k - part.begin) * tile
            got = got_ref[:, at : at + tile].astype(F32)
            acc[piece, :, spot] = acc[piece, :, spot] + got


def start_kernel(parts, tile, me_ref, tgt_ref, *refs):
    acc = refs[-1]
    acc[...] = jnp.zeros_like(acc)
    add_products(acc, tgt_ref, me_ref[0], parts, refs[:-1], tile)


def start_near(parts, me, tgt, got, pieces, width, tile):
    return pl.pallas_call(
        functools.partial(start_kernel, parts, tile),
        out_shape=jax.ShapeDtypeStruct((pieces, got[0].shape[0], width), F32),
        in_specs=[SMEM, SMEM] + [VMEM] * len(got),
        out_specs=VMEM,
        cost_estimate=LONG,
        compiler_params=pltpu.CompilerParams(vmem_limit_bytes=16 * 2**20),
    )(me, tgt, *got)


def far_kernel(groups, count, me_ref, node_ref, *refs):
    head_refs = refs[:groups]
    edge_ref, coupling_ref, basis_ref, near_ref, out_ref, exact, low, high = refs[groups:]
    tgt_tiles, rank, tile = basis_ref.shape
    per = coupling_ref.shape[2] // rank
    pieces, nrhs, width = out_ref.shape
    leaves = width // tile
    for m in range(groups):
        end = head_refs[m].shape[1] - count
        pair = head_refs[m][:, end - 2 * rank : end].astype(F32)
        exact[groups - 1 + (me_ref[0] ^ m)] = pair[:, :rank] + pair[:, rank:]
    for n in range(groups - 2, -1, -1):
        pair = jnp.concatenate([exact[2 * n + 1], exact[2 * n + 2]], axis=1)
        exact[n] = lax.dot_general(
            pair, edge_ref[n], NT, precision=lax.Precision.HIGHEST, preferred_element_type=F32
        )
    zero = jnp.zeros((nrhs, rank), BF16)
    for n in range(2 * groups - 1):
        node = exact[n].astype(BF16)
        low[n] = jnp.concatenate([node, zero], axis=1)
        high[n] = jnp.concatenate([zero, node], axis=1)

    @pl.loop(0, pieces // FAR_PIECES)
    def _(block):
        first = block * FAR_PIECES
        zs = []
        for i in range(FAR_PIECES * leaves):
            tau = first * leaves + i
            nodes = [node_ref[tau * per + k] for k in range(per)]
            stacked = jnp.concatenate(
                [low[nodes[k]] + high[nodes[k + 1]] for k in range(0, per, 2)], axis=1
            )
            z = lax.dot_general(stacked, coupling_ref[tau], NT, preferred_element_type=F32)
            zs.append(z.astype(BF16))
        for i in range(FAR_PIECES * leaves):
            far = jnp.dot(zs[i], basis_ref[first * leaves + i], preferred_element_type=F32)
            p, at = first + i // leaves, slice(i % leaves * tile, (i % leaves + 1) * tile)
            out_ref[p, :, at] = near_ref[p, :, at] + far


def far_field(me, far_node, heads, transfer, coupling, target_basis, near, count):
    groups = len(heads)
    rank = target_basis.shape[1]
    nrhs = near.shape[1]
    nodes = 2 * groups - 1
    return pl.pallas_call(
        functools.partial(far_kernel, groups, count),
        out_shape=jax.ShapeDtypeStruct(near.shape, F32),
        in_specs=[SMEM, SMEM] + [VMEM] * (groups + 4),
        out_specs=VMEM,
        scratch_shapes=[
            pltpu.VMEM((nodes, nrhs, rank), F32),
            pltpu.VMEM((nodes, nrhs, 2 * rank), BF16),
            pltpu.VMEM((nodes, nrhs, 2 * rank), BF16),
        ],
        input_output_aliases={groups + 5: 0},
        compiler_params=pltpu.CompilerParams(vmem_limit_bytes=16 * 2**20),
    )(me, far_node, *heads, transfer, coupling, target_basis, near)


def gather_kernel(parts, tile, me_ref, tgt_ref, far_ref, *refs):
    got_refs, (acc, first_ref, rest_ref) = refs[:-3], refs[-3:]
    add_products(acc, tgt_ref, me_ref[0], parts, got_refs, tile)
    z, core = me_ref[1] // 2, me_ref[1] % 2
    chips = acc.shape[0] // 2
    for n in range(chips):
        m = chips - 1 - 2 * n if n < chips // 2 else 2 * (chips - 1 - n)
        out = first_ref.at[n] if n < chips // 2 else rest_ref.at[n - chips // 2]
        out[...] = acc[2 * (z ^ m) + 1 - core].astype(BF16)


def gather_near(parts, me, tgt, far, got, tile):
    pieces, rows, width = far.shape
    return pl.pallas_call(
        functools.partial(gather_kernel, parts, tile),
        out_shape=[
            jax.ShapeDtypeStruct(far.shape, F32),
            jax.ShapeDtypeStruct((pieces // 4, rows, width), BF16),
            jax.ShapeDtypeStruct((pieces // 4, rows, width), BF16),
        ],
        in_specs=[SMEM] * 2 + [VMEM] * (1 + len(got)),
        out_specs=[VMEM] * 3,
        input_output_aliases={2: 0},
        compiler_params=pltpu.CompilerParams(vmem_limit_bytes=16 * 2**20),
    )(me, tgt, far, *got)


def split_kernel(masks, me_ref, acc_ref, got_ref, *out_refs):
    z, core = me_ref[0] // 2, me_ref[0] % 2
    for n, (m, out_ref) in enumerate(zip(masks, out_refs)):
        out_ref[...] = (acc_ref[2 * (z ^ m) + core] + got_ref[n].astype(F32)).astype(out_ref.dtype)


def split(masks, dtypes, me, acc, got):
    return pl.pallas_call(
        functools.partial(split_kernel, masks),
        out_shape=[jax.ShapeDtypeStruct(got.shape[-2:], d) for d in dtypes],
        in_specs=[SMEM, VMEM, VMEM],
        out_specs=[VMEM] * len(masks),
        compiler_params=pltpu.CompilerParams(vmem_limit_bytes=16 * 2**20),
    )(me, acc, got)


def place_kernel(masks, me_ref, *refs):
    piece_refs, (out_ref, sems) = refs[: len(masks)], refs[-2:]
    copies = []
    for n, (m, piece_ref) in enumerate(zip(masks, piece_refs)):
        width = piece_ref.shape[1]
        spot = pl.ds(pl.multiple_of((me_ref[0] ^ m) * width, width), width)
        copies.append(pltpu.make_async_copy(piece_ref, out_ref.at[:, spot], sems.at[n]))
    for copy in copies:
        copy.start()
    for copy in copies:
        copy.wait()


def place(masks, me, parts, count, out=None):
    rows, width = parts[0].shape
    return pl.pallas_call(
        functools.partial(place_kernel, masks),
        out_shape=jax.ShapeDtypeStruct((rows, width * count), BF16),
        in_specs=[SMEM] + [VMEM] * len(parts) + [ANY] * (out is not None),
        out_specs=ANY,
        scratch_shapes=[pltpu.SemaphoreType.DMA((len(parts),))],
        input_output_aliases={} if out is None else {len(parts) + 1: 0},
        cost_estimate=LONG if out is None else None,
        compiler_params=pltpu.CompilerParams(vmem_limit_bytes=16 * 2**20),
    )(me, *parts, *(() if out is None else (out,)))


def swap(value, axis, mask):
    size = lax.axis_size(axis)
    return lax.ppermute(value, axis, [(i, i ^ mask) for i in range(size)])


def tied(value, *others):
    return lax.optimization_barrier((value,) + others)[0]


def sum_and_share(me, acc, got_first, got_rest):
    chips = acc.shape[0] // 2
    if chips == 4:
        first, near = split((3, 1), (BF16, BF16), me, acc, got_first)
        cross, own = split((2, 0), (F32, F32), me, acc, got_rest)
        a = swap(first, "src", 2)
        cross = (cross + a.astype(F32)).astype(BF16)
        b = swap(cross, "src", 4)
        c = swap(near, "src", 2)
        own = (own + b.astype(F32) + c.astype(F32)).astype(BF16)
        d = swap(own, "src", 4)
        e = swap(own, "src", 2)
        return (0, 1, 2, 3), [own, e, d, swap(d, "src", 2)]
    masks = tuple(range(chips))
    odd, even = masks[::-2], masks[-2::-2]
    first = split(odd, (BF16,) * len(odd), me, acc, got_first)
    *rest, own = split(even, (BF16,) * (len(even) - 1) + (F32,), me, acc, got_rest)
    for m, part in zip(odd + even[:-1], [*first, *rest]):
        own = own + swap(part, "src", 2 * m).astype(F32)
    own = own.astype(BF16)
    return masks, [own] + [swap(own, "src", 2 * m) for m in masks[1:]]


def shards(
    charges, near_tiles, near_tgt, near_src, leaf_basis, transfer, coupling, far_node, target_basis
):
    groups = lax.axis_size("tgt")
    sources = lax.axis_size("src")
    me_t = lax.axis_index("tgt").astype(jnp.int32)
    me_s = lax.axis_index("src").astype(jnp.int32)
    count, tile, _ = near_tiles.shape
    slots = count // groups
    x = charges.T
    me = me_t.reshape(1)

    masks = sorted(range(groups), key=lambda m: -bin(m).count("1"))
    ends = [min(FIRST_HEAD, slots)] + [min(HEAD, slots)] * (groups - 2) + [slots]
    heads = [Part(m, slots, 0, e, True) for m, e in zip(masks, ends)]
    tails = [Part(m, slots, e, slots, False) for m, e in zip(masks, ends) if e < slots]
    first = near_products(heads[:1], me, near_src, near_tgt, x, leaf_basis, near_tiles)
    rest = near_products(
        heads[1:] + tails, me, near_src, near_tgt, tied(x, *first), leaf_basis, near_tiles
    )
    parts = heads + tails
    got = {
        part: swap(y, "tgt", part.mask) if part.mask else y
        for part, y in zip(parts, [*first, *rest])
    }
    by_mask = {part.mask: got[part] for part in heads}

    def targets(some):
        rows = [by_mask[part.mask][:1, -count:] for part in some]
        return jnp.concatenate(rows).astype(F32).astype(jnp.int32)

    early = [part for part in heads if part.mask in (masks[0], masks[-1])]
    late = [part for part in parts if part not in early]
    acc = start_near(
        early,
        me,
        targets(early),
        [got[part] for part in early],
        sources,
        target_basis.shape[0] // sources * tile,
        tile,
    )
    acc = far_field(
        me,
        far_node[0].reshape(-1),
        [by_mask[m] for m in range(groups)],
        transfer[0],
        coupling[0],
        target_basis,
        acc,
        count,
    )
    here = jnp.stack([me_t, me_s])
    acc, first, rest = gather_near(
        late, here, targets(late), acc, [got[part] for part in late], tile
    )
    owners, mine = sum_and_share(
        me_s.reshape(1), acc, swap(first, "src", 1), swap(rest, "src", 1)
    )
    other = [swap(p, "src", 1) for p in mine]
    parts = [(2 * m, q) for m, q in zip(owners, mine)]
    parts += [(2 * m + 1, q) for m, q in zip(owners, other)]
    early = [part for part in parts if part[0] // 2 != owners[-1]]
    late = [part for part in parts if part[0] // 2 == owners[-1]]
    out = None
    for some in (early, late):
        spots, values = zip(*some)
        out = place(spots, me_s.reshape(1), values, sources, out)
    return out.T


def solution(mesh):
    in_specs = (
        P(("src", "tgt"), None),
        P(("src", "tgt"), None, None),
        P(("src", "tgt")),
        P(("src", "tgt")),
        P(("src", "tgt"), None, None),
        P("src", None, None, None),
        P("src", "tgt", None, None),
        P("src", "tgt", None),
        P("tgt", None, None),
    )
    out_specs = P("tgt", None)
    return jax.shard_map(shards, mesh=mesh, in_specs=in_specs, out_specs=out_specs, check_vma=False)
```

```python
import functools
import typing

import jax
import jax.numpy as jnp
from jax import lax
from jax.experimental import pallas as pl
from jax.experimental.pallas import tpu as pltpu
from jax.sharding import PartitionSpec as P

STEP = 8
HEAD = 8
FIRST_HEAD = 32
FAR_PIECES = 2
HALVES = 2
NEAR_VMEM = 60
F32, BF16 = jnp.float32, jnp.bfloat16
NT = (((1,), (1,)), ((), ()))
SMEM = pl.BlockSpec(memory_space=pltpu.SMEM)
LONG = pl.CostEstimate(flops=2**36, bytes_accessed=2**24, transcendentals=0)
VMEM = pl.BlockSpec(memory_space=pltpu.VMEM)
ANY = pl.BlockSpec(memory_space=pl.ANY)


class Part(typing.NamedTuple):
    mask: int
    slots: int
    begin: int
    end: int
    head: bool


def near_kernel(parts, me_ref, src_ref, tgt_ref, x_hbm, basis_ref, tiles_ref, *refs):
    outs, (x_ref, basis, held, sems) = refs[: len(parts)], refs[len(parts) :]
    tile = held.shape[1]
    leaves, rank, _ = basis.shape
    nrhs = x_ref.shape[0]
    count = tiles_ref.shape[0]
    slots = parts[0].slots
    extra = [
        pltpu.make_async_copy(x_hbm, x_ref, sems.at[0]),
        pltpu.make_async_copy(basis_ref, basis, sems.at[1]),
    ]
    copies, spans, at = [], [], 0
    for part in parts:
        first = (me_ref[0] ^ part.mask) * slots
        for k in range(part.begin, part.end, STEP):
            size = min(STEP, part.end - k)
            spans.append((part, k, size, at))
            copies.append(
                pltpu.make_async_copy(
                    tiles_ref.at[pl.ds(first + k, size)],
                    held.at[pl.ds(at, size)],
                    sems.at[2 + len(copies)],
                )
            )
            at += size
    for copy in extra + copies:
        copy.start()
    for copy in extra:
        copy.wait()
    if any(part.head for part in parts):
        root = jnp.zeros((nrhs, rank), F32)
        for i in range(leaves):
            root += lax.dot_general(
                x_ref[:, i * tile : (i + 1) * tile], basis[i], NT, preferred_element_type=F32
            )
        high = root.astype(BF16)
        low = (root - high.astype(F32)).astype(BF16)
        roots = jnp.concatenate([high, low], axis=1)
        tgt = jnp.broadcast_to(tgt_ref[...].astype(F32).astype(BF16), (nrhs, count))
        for part, out in zip(parts, outs):
            if part.head:
                end = out.shape[1] - count
                out[:, end - 2 * rank : end] = roots
                out[:, end:] = tgt
    for (part, begin, size, at), copy in zip(spans, copies):
        copy.wait()
        first = (me_ref[0] ^ part.mask) * slots
        out = outs[parts.index(part)]
        for k in range(size):
            leaf = src_ref[first + begin + k]
            x = x_ref[:, pl.ds(pl.multiple_of(leaf * tile, tile), tile)]
            y = lax.dot_general(x, held[at + k], NT, preferred_element_type=F32)
            spot = (begin - part.begin + k) * tile
            out[:, spot : spot + tile] = y.astype(BF16)


def near_products(parts, me, near_src, near_tgt, x, basis, tiles):
    count, tile, _ = tiles.shape
    nrhs, rank = x.shape[0], basis.shape[1]
    widths = [(p.end - p.begin) * tile + (2 * rank + count if p.head else 0) for p in parts]
    blocks = sum(-(-(p.end - p.begin) // STEP) for p in parts)
    return pl.pallas_call(
        functools.partial(near_kernel, parts),
        out_shape=[jax.ShapeDtypeStruct((nrhs, w), BF16) for w in widths],
        in_specs=[SMEM, SMEM, VMEM, ANY, ANY, ANY],
        out_specs=[VMEM] * len(widths),
        scratch_shapes=[
            pltpu.VMEM(x.shape, BF16),
            pltpu.VMEM(basis.shape, BF16),
            pltpu.VMEM((sum(p.end - p.begin for p in parts), tile, tile), BF16),
            pltpu.SemaphoreType.DMA((blocks + 2,)),
        ],
        compiler_params=pltpu.CompilerParams(vmem_limit_bytes=NEAR_VMEM * 2**20),
    )(me, near_src, near_tgt.reshape(1, count), x, basis, tiles)


def add_products(acc, tgt_ref, me, parts, got_refs, tile):
    leaves = acc.shape[2] // tile
    for n, (part, got_ref) in enumerate(zip(parts, got_refs)):
        for k in range(part.begin, part.end):
            leaf = tgt_ref[n, me * part.slots + k]
            piece = leaf // leaves
            spot = pl.ds(pl.multiple_of((leaf - piece * leaves) * tile, tile), tile)
            at = (k - part.begin) * tile
            got = got_ref[:, at : at + tile].astype(F32)
            acc[piece, :, spot] = acc[piece, :, spot] + got


def start_kernel(parts, tile, me_ref, tgt_ref, *refs):
    acc = refs[-1]
    acc[...] = jnp.zeros_like(acc)
    add_products(acc, tgt_ref, me_ref[0], parts, refs[:-1], tile)


def start_near(parts, me, tgt, got, pieces, width, tile):
    return pl.pallas_call(
        functools.partial(start_kernel, parts, tile),
        out_shape=jax.ShapeDtypeStruct((pieces, got[0].shape[0], width), F32),
        in_specs=[SMEM, SMEM] + [VMEM] * len(got),
        out_specs=VMEM,
        cost_estimate=LONG,
        compiler_params=pltpu.CompilerParams(vmem_limit_bytes=16 * 2**20),
    )(me, tgt, *got)


def far_kernel(groups, count, me_ref, node_ref, *refs):
    head_refs = refs[:groups]
    edge_ref, coupling_ref, basis_ref, near_ref, out_ref, exact, low, high = refs[groups:]
    tgt_tiles, rank, tile = basis_ref.shape
    per = coupling_ref.shape[2] // rank
    pieces, nrhs, width = out_ref.shape
    leaves = width // tile
    for m in range(groups):
        end = head_refs[m].shape[1] - count
        pair = head_refs[m][:, end - 2 * rank : end].astype(F32)
        exact[groups - 1 + (me_ref[0] ^ m)] = pair[:, :rank] + pair[:, rank:]
    for n in range(groups - 2, -1, -1):
        pair = jnp.concatenate([exact[2 * n + 1], exact[2 * n + 2]], axis=1)
        exact[n] = lax.dot_general(
            pair, edge_ref[n], NT, precision=lax.Precision.HIGHEST, preferred_element_type=F32
        )
    zero = jnp.zeros((nrhs, rank), BF16)
    for n in range(2 * groups - 1):
        node = exact[n].astype(BF16)
        low[n] = jnp.concatenate([node, zero], axis=1)
        high[n] = jnp.concatenate([zero, node], axis=1)

    @pl.loop(0, pieces // FAR_PIECES)
    def _(block):
        first = block * FAR_PIECES
        zs = []
        for i in range(FAR_PIECES * leaves):
            tau = first * leaves + i
            nodes = [node_ref[tau * per + k] for k in range(per)]
            stacked = jnp.concatenate(
                [low[nodes[k]] + high[nodes[k + 1]] for k in range(0, per, 2)], axis=1
            )
            z = lax.dot_general(stacked, coupling_ref[tau], NT, preferred_element_type=F32)
            zs.append(z.astype(BF16))
        for i in range(FAR_PIECES * leaves):
            far = jnp.dot(zs[i], basis_ref[first * leaves + i], preferred_element_type=F32)
            p, at = first + i // leaves, slice(i % leaves * tile, (i % leaves + 1) * tile)
            out_ref[p, :, at] = near_ref[p, :, at] + far


def far_field(me, far_node, heads, transfer, coupling, target_basis, near, count):
    groups = len(heads)
    rank = target_basis.shape[1]
    nrhs = near.shape[1]
    nodes = 2 * groups - 1
    return pl.pallas_call(
        functools.partial(far_kernel, groups, count),
        out_shape=jax.ShapeDtypeStruct(near.shape, F32),
        in_specs=[SMEM, SMEM] + [VMEM] * (groups + 4),
        out_specs=VMEM,
        scratch_shapes=[
            pltpu.VMEM((nodes, nrhs, rank), F32),
            pltpu.VMEM((nodes, nrhs, 2 * rank), BF16),
            pltpu.VMEM((nodes, nrhs, 2 * rank), BF16),
        ],
        input_output_aliases={groups + 5: 0},
        compiler_params=pltpu.CompilerParams(vmem_limit_bytes=16 * 2**20),
    )(me, far_node, *heads, transfer, coupling, target_basis, near)


def gather_kernel(parts, tile, me_ref, tgt_ref, far_ref, *refs):
    got_refs, acc, send_refs = refs[: len(parts)], refs[len(parts)], refs[len(parts) + 1 :]
    add_products(acc, tgt_ref, me_ref[0], parts, got_refs, tile)
    core = me_ref[1] % 2
    rows = send_refs[0].shape[1]
    for c, send_ref in enumerate(send_refs):
        for z in range(send_ref.shape[0]):
            send = acc[2 * z + 1 - core, c * rows : (c + 1) * rows]
            send_ref[z] = send.astype(BF16)


def gather_near(parts, me, tgt, far, got, tile):
    pieces, rows, width = far.shape
    return pl.pallas_call(
        functools.partial(gather_kernel, parts, tile),
        out_shape=[
            jax.ShapeDtypeStruct(far.shape, F32),
        ]
        + [jax.ShapeDtypeStruct((pieces // 2, rows // HALVES, width), BF16)] * HALVES,
        in_specs=[SMEM] * 2 + [VMEM] * (1 + len(got)),
        out_specs=[VMEM] * (1 + HALVES),
        input_output_aliases={2: 0},
        compiler_params=pltpu.CompilerParams(vmem_limit_bytes=16 * 2**20),
    )(me, tgt, far, *got)


def split_kernel(half, masks, me_ref, acc_ref, got_ref, *out_refs):
    z, core = me_ref[0] // 2, me_ref[0] % 2
    rows = got_ref.shape[1]
    for m, out_ref in zip(masks, out_refs):
        here = acc_ref[2 * (z ^ m) + core, half * rows : (half + 1) * rows]
        out_ref[...] = (here + got_ref[z ^ m].astype(F32)).astype(out_ref.dtype)


def split(half, masks, dtypes, me, acc, got):
    return pl.pallas_call(
        functools.partial(split_kernel, half, masks),
        out_shape=[jax.ShapeDtypeStruct(got.shape[1:], d) for d in dtypes],
        in_specs=[SMEM, VMEM, VMEM],
        out_specs=[VMEM] * len(masks),
        compiler_params=pltpu.CompilerParams(vmem_limit_bytes=16 * 2**20),
    )(me, acc, got)


def place_kernel(masks, me_ref, *refs):
    piece_refs, (out_ref, sems) = refs[: len(masks)], refs[-2:]
    copies = []
    for n, ((half, m), piece_ref) in enumerate(zip(masks, piece_refs)):
        rows, width = piece_ref.shape
        spot = pl.ds(pl.multiple_of((me_ref[0] ^ m) * width, width), width)
        out = out_ref.at[pl.ds(half * rows, rows), spot]
        copies.append(pltpu.make_async_copy(piece_ref, out, sems.at[n]))
    for copy in copies:
        copy.start()
    for copy in copies:
        copy.wait()


def place(masks, me, parts, count, out=None):
    rows, width = parts[0].shape
    return pl.pallas_call(
        functools.partial(place_kernel, masks),
        out_shape=jax.ShapeDtypeStruct((HALVES * rows, width * count), BF16),
        in_specs=[SMEM] + [VMEM] * len(parts) + [ANY] * (out is not None),
        out_specs=ANY,
        scratch_shapes=[pltpu.SemaphoreType.DMA((len(parts),))],
        input_output_aliases={} if out is None else {len(parts) + 1: 0},
        cost_estimate=LONG if out is None else None,
        compiler_params=pltpu.CompilerParams(vmem_limit_bytes=16 * 2**20),
    )(me, *parts, *(() if out is None else (out,)))


def swap(value, axis, mask):
    size = lax.axis_size(axis)
    return lax.ppermute(value, axis, [(i, i ^ mask) for i in range(size)])


def tied(value, *others):
    return lax.optimization_barrier((value,) + others)[0]


def sum_and_share(half, me, acc, got):
    chips = acc.shape[0] // 2
    if chips == 4:
        first, near, cross, own = split(half, (3, 1, 2, 0), (BF16, BF16, F32, F32), me, acc, got)
        a = swap(first, "src", 2)
        cross = (cross + a.astype(F32)).astype(BF16)
        b = swap(cross, "src", 4)
        c = swap(tied(near, cross), "src", 2)
        own = own + b.astype(F32)
        own = (own + c.astype(F32)).astype(BF16)
        d = swap(own, "src", 4)
        e = swap(own, "src", 2)
        return (0, 1, 2, 3), [own, e, d, swap(d, "src", 2)]
    masks = tuple(range(chips))
    dtypes = (F32,) + (BF16,) * (chips - 1)
    own, *rest = split(half, masks, dtypes, me, acc, got)
    for m, part in zip(masks[1:], rest):
        own = own + swap(part, "src", 2 * m).astype(F32)
    own = own.astype(BF16)
    return masks, [own] + [swap(own, "src", 2 * m) for m in masks[1:]]


def shards(
    charges, near_tiles, near_tgt, near_src, leaf_basis, transfer, coupling, far_node, target_basis
):
    groups = lax.axis_size("tgt")
    sources = lax.axis_size("src")
    me_t = lax.axis_index("tgt").astype(jnp.int32)
    me_s = lax.axis_index("src").astype(jnp.int32)
    count, tile, _ = near_tiles.shape
    slots = count // groups
    x = charges.T
    me = me_t.reshape(1)

    masks = sorted(range(groups), key=lambda m: -bin(m).count("1"))
    ends = [min(FIRST_HEAD, slots)] + [min(HEAD, slots)] * (groups - 2) + [slots]
    heads = [Part(m, slots, 0, e, True) for m, e in zip(masks, ends)]
    tails = [Part(m, slots, e, slots, False) for m, e in zip(masks, ends) if e < slots]
    first = near_products(heads[:1], me, near_src, near_tgt, x, leaf_basis, near_tiles)
    rest = near_products(
        heads[1:] + tails, me, near_src, near_tgt, tied(x, *first), leaf_basis, near_tiles
    )
    parts = heads + tails
    got = {
        part: swap(y, "tgt", part.mask) if part.mask else y
        for part, y in zip(parts, [*first, *rest])
    }
    by_mask = {part.mask: got[part] for part in heads}

    def targets(some):
        rows = [by_mask[part.mask][:1, -count:] for part in some]
        return jnp.concatenate(rows).astype(F32).astype(jnp.int32)

    early = [part for part in heads if part.mask in (masks[0], masks[-1])]
    late = [part for part in parts if part not in early]
    acc = start_near(
        early,
        me,
        targets(early),
        [got[part] for part in early],
        sources,
        target_basis.shape[0] // sources * tile,
        tile,
    )
    acc = far_field(
        me,
        far_node[0].reshape(-1),
        [by_mask[m] for m in range(groups)],
        transfer[0],
        coupling[0],
        target_basis,
        acc,
        count,
    )
    here = jnp.stack([me_t, me_s])
    acc, *sends = gather_near(
        late, here, targets(late), acc, [got[part] for part in late], tile
    )
    me = me_s.reshape(1)
    parts = []
    for half, send in enumerate(sends):
        owners, mine = sum_and_share(half, me, acc, swap(send, "src", 1))
        parts += [((half, 2 * m), q) for m, q in zip(owners, mine)]
        parts += [((half, 2 * m + 1), swap(q, "src", 1)) for m, q in zip(owners, mine)]
    last = parts[-len(owners) - 1], parts[-1]
    out = None
    for some in ([part for part in parts if part[0] not in (last[0][0], last[1][0])], last):
        spots, values = zip(*some)
        out = place(spots, me, values, sources, out)
    return out.T


def solution(mesh):
    in_specs = (
        P(("src", "tgt"), None),
        P(("src", "tgt"), None, None),
        P(("src", "tgt")),
        P(("src", "tgt")),
        P(("src", "tgt"), None, None),
        P("src", None, None, None),
        P("src", "tgt", None, None),
        P("src", "tgt", None),
        P("tgt", None, None),
    )
    out_specs = P("tgt", None)
    return jax.shard_map(shards, mesh=mesh, in_specs=in_specs, out_specs=out_specs, check_vma=False)
```

```python
import functools
import typing

import jax
import jax.numpy as jnp
from jax import lax
from jax.experimental import pallas as pl
from jax.experimental.pallas import tpu as pltpu
from jax.sharding import PartitionSpec as P

STEP = 32
HEAD = 4
FIRST_HEAD = 32
FAR_PIECES = 4
HALVES = 2
NEAR_VMEM = 60
F32, BF16 = jnp.float32, jnp.bfloat16
NT = (((1,), (1,)), ((), ()))
SMEM = pl.BlockSpec(memory_space=pltpu.SMEM)
LONG = pl.CostEstimate(flops=2**36, bytes_accessed=2**24, transcendentals=0)
VMEM = pl.BlockSpec(memory_space=pltpu.VMEM)
ANY = pl.BlockSpec(memory_space=pl.ANY)


class Part(typing.NamedTuple):
    mask: int
    slots: int
    begin: int
    end: int
    head: bool


def near_kernel(parts, me_ref, src_ref, tgt_ref, x_hbm, basis_ref, tiles_ref, *refs):
    outs, (x_ref, basis, held, sems) = refs[: len(parts)], refs[len(parts) :]
    tile = held.shape[1]
    leaves, rank, _ = basis.shape
    nrhs = x_ref.shape[0]
    count = tiles_ref.shape[0]
    slots = parts[0].slots
    extra = [
        pltpu.make_async_copy(x_hbm, x_ref, sems.at[0]),
        pltpu.make_async_copy(basis_ref, basis, sems.at[1]),
    ]
    copies, spans, at = [], [], 0
    for part in parts:
        first = (me_ref[0] ^ part.mask) * slots
        for k in range(part.begin, part.end, STEP):
            size = min(STEP, part.end - k)
            spans.append((part, k, size, at))
            copies.append(
                pltpu.make_async_copy(
                    tiles_ref.at[pl.ds(first + k, size)],
                    held.at[pl.ds(at, size)],
                    sems.at[2 + len(copies)],
                )
            )
            at += size
    for copy in extra + copies:
        copy.start()
    for copy in extra:
        copy.wait()
    if any(part.head for part in parts):
        root = jnp.zeros((nrhs, rank), F32)
        for i in range(leaves):
            root += lax.dot_general(
                x_ref[:, i * tile : (i + 1) * tile], basis[i], NT, preferred_element_type=F32
            )
        high = root.astype(BF16)
        low = (root - high.astype(F32)).astype(BF16)
        roots = jnp.concatenate([high, low], axis=1)
        tgt = jnp.broadcast_to(tgt_ref[...].astype(F32).astype(BF16), (nrhs, count))
        for part, out in zip(parts, outs):
            if part.head:
                end = out.shape[1] - count
                out[:, end - 2 * rank : end] = roots
                out[:, end:] = tgt
    for (part, begin, size, at), copy in zip(spans, copies):
        copy.wait()
        first = (me_ref[0] ^ part.mask) * slots
        out = outs[parts.index(part)]
        for k in range(size):
            leaf = src_ref[first + begin + k]
            x = x_ref[:, pl.ds(pl.multiple_of(leaf * tile, tile), tile)]
            y = lax.dot_general(x, held[at + k], NT, preferred_element_type=F32)
            spot = (begin - part.begin + k) * tile
            out[:, spot : spot + tile] = y.astype(BF16)


def near_products(parts, me, near_src, near_tgt, x, basis, tiles):
    count, tile, _ = tiles.shape
    nrhs, rank = x.shape[0], basis.shape[1]
    widths = [(p.end - p.begin) * tile + (2 * rank + count if p.head else 0) for p in parts]
    blocks = sum(-(-(p.end - p.begin) // STEP) for p in parts)
    return pl.pallas_call(
        functools.partial(near_kernel, parts),
        out_shape=[jax.ShapeDtypeStruct((nrhs, w), BF16) for w in widths],
        in_specs=[SMEM, SMEM, VMEM, ANY, ANY, ANY],
        out_specs=[VMEM] * len(widths),
        scratch_shapes=[
            pltpu.VMEM(x.shape, BF16),
            pltpu.VMEM(basis.shape, BF16),
            pltpu.VMEM((sum(p.end - p.begin for p in parts), tile, tile), BF16),
            pltpu.SemaphoreType.DMA((blocks + 2,)),
        ],
        compiler_params=pltpu.CompilerParams(vmem_limit_bytes=NEAR_VMEM * 2**20),
    )(me, near_src, near_tgt.reshape(1, count), x, basis, tiles)


def add_products(acc, tgt_ref, me, parts, got_refs, tile):
    leaves = acc.shape[2] // tile
    for n, (part, got_ref) in enumerate(zip(parts, got_refs)):
        for k in range(part.begin, part.end):
            leaf = tgt_ref[n, me * part.slots + k]
            piece = leaf // leaves
            spot = pl.ds(pl.multiple_of((leaf - piece * leaves) * tile, tile), tile)
            at = (k - part.begin) * tile
            got = got_ref[:, at : at + tile].astype(F32)
            acc[piece, :, spot] = acc[piece, :, spot] + got


def start_kernel(parts, tile, me_ref, tgt_ref, *refs):
    acc = refs[-1]
    acc[...] = jnp.zeros_like(acc)
    add_products(acc, tgt_ref, me_ref[0], parts, refs[:-1], tile)


def start_near(parts, me, tgt, got, pieces, width, tile):
    return pl.pallas_call(
        functools.partial(start_kernel, parts, tile),
        out_shape=jax.ShapeDtypeStruct((pieces, got[0].shape[0], width), F32),
        in_specs=[SMEM, SMEM] + [VMEM] * len(got),
        out_specs=VMEM,
        cost_estimate=LONG,
        compiler_params=pltpu.CompilerParams(vmem_limit_bytes=16 * 2**20),
    )(me, tgt, *got)


def far_kernel(groups, count, me_ref, node_ref, *refs):
    head_refs = refs[:groups]
    edge_ref, coupling_ref, basis_ref, near_ref, out_ref, exact, low, high = refs[groups:]
    tgt_tiles, rank, tile = basis_ref.shape
    per = coupling_ref.shape[2] // rank
    pieces, nrhs, width = out_ref.shape
    leaves = width // tile
    for m in range(groups):
        end = head_refs[m].shape[1] - count
        pair = head_refs[m][:, end - 2 * rank : end].astype(F32)
        exact[groups - 1 + (me_ref[0] ^ m)] = pair[:, :rank] + pair[:, rank:]
    for n in range(groups - 2, -1, -1):
        pair = jnp.concatenate([exact[2 * n + 1], exact[2 * n + 2]], axis=1)
        exact[n] = lax.dot_general(
            pair, edge_ref[n], NT, precision=lax.Precision.HIGHEST, preferred_element_type=F32
        )
    zero = jnp.zeros((nrhs, rank), BF16)
    for n in range(2 * groups - 1):
        node = exact[n].astype(BF16)
        low[n] = jnp.concatenate([node, zero], axis=1)
        high[n] = jnp.concatenate([zero, node], axis=1)

    @pl.loop(0, pieces // FAR_PIECES)
    def _(block):
        first = block * FAR_PIECES
        zs = []
        for i in range(FAR_PIECES * leaves):
            tau = first * leaves + i
            nodes = [node_ref[tau * per + k] for k in range(per)]
            stacked = jnp.concatenate(
                [low[nodes[k]] + high[nodes[k + 1]] for k in range(0, per, 2)], axis=1
            )
            z = lax.dot_general(stacked, coupling_ref[tau], NT, preferred_element_type=F32)
            zs.append(z.astype(BF16))
        for i in range(FAR_PIECES * leaves):
            far = jnp.dot(zs[i], basis_ref[first * leaves + i], preferred_element_type=F32)
            p, at = first + i // leaves, slice(i % leaves * tile, (i % leaves + 1) * tile)
            out_ref[p, :, at] = near_ref[p, :, at] + far


def far_field(me, far_node, heads, transfer, coupling, target_basis, near, count):
    groups = len(heads)
    rank = target_basis.shape[1]
    nrhs = near.shape[1]
    nodes = 2 * groups - 1
    return pl.pallas_call(
        functools.partial(far_kernel, groups, count),
        out_shape=jax.ShapeDtypeStruct(near.shape, F32),
        in_specs=[SMEM, SMEM] + [VMEM] * (groups + 4),
        out_specs=VMEM,
        scratch_shapes=[
            pltpu.VMEM((nodes, nrhs, rank), F32),
            pltpu.VMEM((nodes, nrhs, 2 * rank), BF16),
            pltpu.VMEM((nodes, nrhs, 2 * rank), BF16),
        ],
        input_output_aliases={groups + 5: 0},
        compiler_params=pltpu.CompilerParams(vmem_limit_bytes=16 * 2**20),
    )(me, far_node, *heads, transfer, coupling, target_basis, near)


def gather_kernel(parts, tile, me_ref, tgt_ref, far_ref, *refs):
    got_refs, acc, send_refs = refs[: len(parts)], refs[len(parts)], refs[len(parts) + 1 :]
    add_products(acc, tgt_ref, me_ref[0], parts, got_refs, tile)
    core = me_ref[1] % 2
    rows = send_refs[0].shape[1]
    for c, send_ref in enumerate(send_refs):
        for z in range(send_ref.shape[0]):
            send = acc[2 * z + 1 - core, c * rows : (c + 1) * rows]
            send_ref[z] = send.astype(BF16)


def gather_near(parts, me, tgt, far, got, tile):
    pieces, rows, width = far.shape
    return pl.pallas_call(
        functools.partial(gather_kernel, parts, tile),
        out_shape=[
            jax.ShapeDtypeStruct(far.shape, F32),
        ]
        + [jax.ShapeDtypeStruct((pieces // 2, rows // HALVES, width), BF16)] * HALVES,
        in_specs=[SMEM] * 2 + [VMEM] * (1 + len(got)),
        out_specs=[VMEM] * (1 + HALVES),
        input_output_aliases={2: 0},
        compiler_params=pltpu.CompilerParams(vmem_limit_bytes=16 * 2**20),
    )(me, tgt, far, *got)


def split_kernel(half, masks, me_ref, acc_ref, got_ref, *out_refs):
    z, core = me_ref[0] // 2, me_ref[0] % 2
    rows = got_ref.shape[1]
    for m, out_ref in zip(masks, out_refs):
        here = acc_ref[2 * (z ^ m) + core, half * rows : (half + 1) * rows]
        out_ref[...] = (here + got_ref[z ^ m].astype(F32)).astype(out_ref.dtype)


def split(half, masks, dtypes, me, acc, got):
    return pl.pallas_call(
        functools.partial(split_kernel, half, masks),
        out_shape=[jax.ShapeDtypeStruct(got.shape[1:], d) for d in dtypes],
        in_specs=[SMEM, VMEM, VMEM],
        out_specs=[VMEM] * len(masks),
        compiler_params=pltpu.CompilerParams(vmem_limit_bytes=16 * 2**20),
    )(me, acc, got)


def place_kernel(masks, me_ref, *refs):
    piece_refs, (out_ref, sems) = refs[: len(masks)], refs[-2:]
    copies = []
    for n, ((half, m), piece_ref) in enumerate(zip(masks, piece_refs)):
        rows, width = piece_ref.shape
        spot = pl.ds(pl.multiple_of((me_ref[0] ^ m) * width, width), width)
        out = out_ref.at[pl.ds(half * rows, rows), spot]
        copies.append(pltpu.make_async_copy(piece_ref, out, sems.at[n]))
    for copy in copies:
        copy.start()
    for copy in copies:
        copy.wait()


def place(masks, me, parts, count, out, early):
    rows, width = parts[0].shape
    return pl.pallas_call(
        functools.partial(place_kernel, masks),
        out_shape=jax.ShapeDtypeStruct((HALVES * rows, width * count), BF16),
        in_specs=[SMEM] + [VMEM] * len(parts) + [ANY] * (out is not None),
        out_specs=ANY,
        scratch_shapes=[pltpu.SemaphoreType.DMA((len(parts),))],
        input_output_aliases={} if out is None else {len(parts) + 1: 0},
        cost_estimate=LONG if early else None,
        compiler_params=pltpu.CompilerParams(vmem_limit_bytes=16 * 2**20),
    )(me, *parts, *(() if out is None else (out,)))


def swap(value, axis, mask):
    size = lax.axis_size(axis)
    return lax.ppermute(value, axis, [(i, i ^ mask) for i in range(size)])


def tied(value, *others):
    return lax.optimization_barrier((value,) + others)[0]


def sum_and_share(half, me, acc, got):
    chips = acc.shape[0] // 2
    if chips == 4:
        first, near, cross, own = split(half, (3, 1, 2, 0), (BF16, BF16, F32, F32), me, acc, got)
        a = swap(first, "src", 2)
        cross = (cross + a.astype(F32)).astype(BF16)
        b = swap(cross, "src", 4)
        c = swap(tied(near, cross), "src", 2)
        own = own + b.astype(F32)
        own = (own + c.astype(F32)).astype(BF16)
        d = swap(own, "src", 4)
        e = swap(own, "src", 2)
        return (0, 1, 2, 3), [own, e, d, swap(d, "src", 2)]
    masks = tuple(range(chips))
    dtypes = (F32,) + (BF16,) * (chips - 1)
    own, *rest = split(half, masks, dtypes, me, acc, got)
    for m, part in zip(masks[1:], rest):
        own = own + swap(part, "src", 2 * m).astype(F32)
    own = own.astype(BF16)
    return masks, [own] + [swap(own, "src", 2 * m) for m in masks[1:]]


def shards(
    charges, near_tiles, near_tgt, near_src, leaf_basis, transfer, coupling, far_node, target_basis
):
    groups = lax.axis_size("tgt")
    sources = lax.axis_size("src")
    me_t = lax.axis_index("tgt").astype(jnp.int32)
    me_s = lax.axis_index("src").astype(jnp.int32)
    count, tile, _ = near_tiles.shape
    slots = count // groups
    x = charges.T
    me = me_t.reshape(1)

    masks = sorted(range(groups), key=lambda m: -bin(m).count("1"))
    ends = [min(FIRST_HEAD, slots)] + [min(HEAD, slots)] * (groups - 2) + [slots]
    heads = [Part(m, slots, 0, e, True) for m, e in zip(masks, ends)]
    tails = [Part(m, slots, e, slots, False) for m, e in zip(masks, ends) if e < slots]
    first = near_products(heads[:1], me, near_src, near_tgt, x, leaf_basis, near_tiles)
    rest = near_products(
        heads[1:] + tails, me, near_src, near_tgt, tied(x, *first), leaf_basis, near_tiles
    )
    parts = heads + tails
    got = {
        part: swap(y, "tgt", part.mask) if part.mask else y
        for part, y in zip(parts, [*first, *rest])
    }
    by_mask = {part.mask: got[part] for part in heads}

    def targets(some):
        rows = [by_mask[part.mask][:1, -count:] for part in some]
        return jnp.concatenate(rows).astype(F32).astype(jnp.int32)

    early = [part for part in heads if part.mask in (masks[0], masks[-1])]
    late = [part for part in parts if part not in early]
    acc = start_near(
        early,
        me,
        targets(early),
        [got[part] for part in early],
        sources,
        target_basis.shape[0] // sources * tile,
        tile,
    )
    acc = far_field(
        me,
        far_node[0].reshape(-1),
        [by_mask[m] for m in range(groups)],
        transfer[0],
        coupling[0],
        target_basis,
        acc,
        count,
    )
    here = jnp.stack([me_t, me_s])
    acc, *sends = gather_near(
        late, here, targets(late), acc, [got[part] for part in late], tile
    )
    me = me_s.reshape(1)
    parts = []
    for half, send in enumerate(sends):
        owners, mine = sum_and_share(half, me, acc, swap(send, "src", 1))
        parts += [((half, 2 * m), q) for m, q in zip(owners, mine)]
        parts += [((half, 2 * m + 1), swap(q, "src", 1)) for m, q in zip(owners, mine)]
    last = parts[-len(owners) - 1], parts[-1]
    each = 2 * len(owners)
    steps = [parts[:-each], [part for part in parts[-each:] if part[0] not in dict(last)], last]
    out = None
    for some in steps:
        spots, values = zip(*some)
        out = place(spots, me, values, sources, out, some is not last)
    return out.T


def solution(mesh):
    in_specs = (
        P(("src", "tgt"), None),
        P(("src", "tgt"), None, None),
        P(("src", "tgt")),
        P(("src", "tgt")),
        P(("src", "tgt"), None, None),
        P("src", None, None, None),
        P("src", "tgt", None, None),
        P("src", "tgt", None),
        P("tgt", None, None),
    )
    out_specs = P("tgt", None)
    return jax.shard_map(shards, mesh=mesh, in_specs=in_specs, out_specs=out_specs, check_vma=False)
```

```python
import functools
import typing

import jax
import jax.numpy as jnp
from jax import lax
from jax.experimental import pallas as pl
from jax.experimental.pallas import tpu as pltpu
from jax.sharding import PartitionSpec as P

STEP = 32
HEAD = 4
FIRST_HEAD = 32
FAR_PIECES = 4
HALVES = 2
NEAR_VMEM = 60
F32, BF16 = jnp.float32, jnp.bfloat16
NT = (((1,), (1,)), ((), ()))
SMEM = pl.BlockSpec(memory_space=pltpu.SMEM)
LONG = pl.CostEstimate(flops=2**36, bytes_accessed=2**24, transcendentals=0)
VMEM = pl.BlockSpec(memory_space=pltpu.VMEM)
ANY = pl.BlockSpec(memory_space=pl.ANY)


class Part(typing.NamedTuple):
    mask: int
    slots: int
    begin: int
    end: int
    head: bool


def near_kernel(parts, me_ref, src_ref, tgt_ref, x_hbm, basis_ref, tiles_ref, *refs):
    outs, (x_ref, basis, held, sems) = refs[: len(parts)], refs[len(parts) :]
    tile = held.shape[1]
    leaves, rank, _ = basis.shape
    nrhs = x_ref.shape[0]
    count = tiles_ref.shape[0]
    slots = parts[0].slots
    extra = [
        pltpu.make_async_copy(x_hbm, x_ref, sems.at[0]),
        pltpu.make_async_copy(basis_ref, basis, sems.at[1]),
    ]
    copies, spans, at = [], [], 0
    for part in parts:
        first = (me_ref[0] ^ part.mask) * slots
        for k in range(part.begin, part.end, STEP):
            size = min(STEP, part.end - k)
            spans.append((part, k, size, at))
            copies.append(
                pltpu.make_async_copy(
                    tiles_ref.at[pl.ds(first + k, size)],
                    held.at[pl.ds(at, size)],
                    sems.at[2 + len(copies)],
                )
            )
            at += size
    for copy in extra + copies:
        copy.start()
    for copy in extra:
        copy.wait()
    if any(part.head for part in parts):
        root = jnp.zeros((nrhs, rank), F32)
        for i in range(leaves):
            root += lax.dot_general(
                x_ref[:, i * tile : (i + 1) * tile], basis[i], NT, preferred_element_type=F32
            )
        tgt = tgt_ref[...].astype(F32).astype(BF16)
        rows = nrhs * rank // count
        tgt = [
            jnp.broadcast_to(tgt[:, i : i + rank], (rows, rank)) for i in range(0, count, rank)
        ]
        roots = jnp.concatenate([root.astype(BF16), jnp.concatenate(tgt, axis=0)], axis=1)
        for part, out in zip(parts, outs):
            if part.head:
                out[:, out.shape[1] - 2 * rank :] = roots
    for (part, begin, size, at), copy in zip(spans, copies):
        copy.wait()
        first = (me_ref[0] ^ part.mask) * slots
        out = outs[parts.index(part)]
        for k in range(size):
            leaf = src_ref[first + begin + k]
            x = x_ref[:, pl.ds(pl.multiple_of(leaf * tile, tile), tile)]
            y = lax.dot_general(x, held[at + k], NT, preferred_element_type=F32)
            spot = (begin - part.begin + k) * tile
            out[:, spot : spot + tile] = y.astype(BF16)


def near_products(parts, me, near_src, near_tgt, x, basis, tiles):
    count, tile, _ = tiles.shape
    nrhs, rank = x.shape[0], basis.shape[1]
    widths = [(p.end - p.begin) * tile + (2 * rank if p.head else 0) for p in parts]
    blocks = sum(-(-(p.end - p.begin) // STEP) for p in parts)
    return pl.pallas_call(
        functools.partial(near_kernel, parts),
        out_shape=[jax.ShapeDtypeStruct((nrhs, w), BF16) for w in widths],
        in_specs=[SMEM, SMEM, VMEM, ANY, ANY, ANY],
        out_specs=[VMEM] * len(widths),
        scratch_shapes=[
            pltpu.VMEM(x.shape, BF16),
            pltpu.VMEM(basis.shape, BF16),
            pltpu.VMEM((sum(p.end - p.begin for p in parts), tile, tile), BF16),
            pltpu.SemaphoreType.DMA((blocks + 2,)),
        ],
        compiler_params=pltpu.CompilerParams(vmem_limit_bytes=NEAR_VMEM * 2**20),
    )(me, near_src, near_tgt.reshape(1, count), x, basis, tiles)


def add_products(acc, tgt_ref, me, parts, got_refs, tile):
    leaves = acc.shape[2] // tile
    for n, (part, got_ref) in enumerate(zip(parts, got_refs)):
        for k in range(part.begin, part.end):
            leaf = tgt_ref[n, me * part.slots + k]
            piece = leaf // leaves
            spot = pl.ds(pl.multiple_of((leaf - piece * leaves) * tile, tile), tile)
            at = (k - part.begin) * tile
            got = got_ref[:, at : at + tile].astype(F32)
            acc[piece, :, spot] = acc[piece, :, spot] + got


def start_kernel(parts, tile, me_ref, tgt_ref, *refs):
    acc = refs[-1]
    acc[...] = jnp.zeros_like(acc)
    add_products(acc, tgt_ref, me_ref[0], parts, refs[:-1], tile)


def start_near(parts, me, tgt, got, pieces, width, tile):
    return pl.pallas_call(
        functools.partial(start_kernel, parts, tile),
        out_shape=jax.ShapeDtypeStruct((pieces, got[0].shape[0], width), F32),
        in_specs=[SMEM, SMEM] + [VMEM] * len(got),
        out_specs=VMEM,
        cost_estimate=LONG,
        compiler_params=pltpu.CompilerParams(vmem_limit_bytes=16 * 2**20),
    )(me, tgt, *got)


def far_kernel(groups, me_ref, node_ref, *refs):
    head_refs = refs[:groups]
    edge_ref, coupling_ref, basis_ref, near_ref, out_ref, exact, low, high = refs[groups:]
    tgt_tiles, rank, tile = basis_ref.shape
    per = coupling_ref.shape[2] // rank
    pieces, nrhs, width = out_ref.shape
    leaves = width // tile
    for m in range(groups):
        end = head_refs[m].shape[1] - 2 * rank
        exact[groups - 1 + (me_ref[0] ^ m)] = head_refs[m][:, end : end + rank].astype(F32)
    for n in range(groups - 2, -1, -1):
        pair = jnp.concatenate([exact[2 * n + 1], exact[2 * n + 2]], axis=1)
        exact[n] = lax.dot_general(
            pair, edge_ref[n], NT, precision=lax.Precision.HIGHEST, preferred_element_type=F32
        )
    zero = jnp.zeros((nrhs, rank), BF16)
    for n in range(2 * groups - 1):
        node = exact[n].astype(BF16)
        low[n] = jnp.concatenate([node, zero], axis=1)
        high[n] = jnp.concatenate([zero, node], axis=1)

    @pl.loop(0, pieces // FAR_PIECES)
    def _(block):
        first = block * FAR_PIECES
        zs = []
        for i in range(FAR_PIECES * leaves):
            tau = first * leaves + i
            nodes = [node_ref[tau * per + k] for k in range(per)]
            stacked = jnp.concatenate(
                [low[nodes[k]] + high[nodes[k + 1]] for k in range(0, per, 2)], axis=1
            )
            z = lax.dot_general(stacked, coupling_ref[tau], NT, preferred_element_type=F32)
            zs.append(z.astype(BF16))
        for i in range(FAR_PIECES * leaves):
            far = jnp.dot(zs[i], basis_ref[first * leaves + i], preferred_element_type=F32)
            p, at = first + i // leaves, slice(i % leaves * tile, (i % leaves + 1) * tile)
            out_ref[p, :, at] = near_ref[p, :, at] + far


def far_field(me, far_node, heads, transfer, coupling, target_basis, near):
    groups = len(heads)
    rank = target_basis.shape[1]
    nrhs = near.shape[1]
    nodes = 2 * groups - 1
    return pl.pallas_call(
        functools.partial(far_kernel, groups),
        out_shape=jax.ShapeDtypeStruct(near.shape, F32),
        in_specs=[SMEM, SMEM] + [VMEM] * (groups + 4),
        out_specs=VMEM,
        scratch_shapes=[
            pltpu.VMEM((nodes, nrhs, rank), F32),
            pltpu.VMEM((nodes, nrhs, 2 * rank), BF16),
            pltpu.VMEM((nodes, nrhs, 2 * rank), BF16),
        ],
        input_output_aliases={groups + 5: 0},
        compiler_params=pltpu.CompilerParams(vmem_limit_bytes=16 * 2**20),
    )(me, far_node, *heads, transfer, coupling, target_basis, near)


def gather_kernel(parts, tile, me_ref, tgt_ref, far_ref, *refs):
    got_refs, acc, send_refs = refs[: len(parts)], refs[len(parts)], refs[len(parts) + 1 :]
    add_products(acc, tgt_ref, me_ref[0], parts, got_refs, tile)
    core = me_ref[1] % 2
    rows = send_refs[0].shape[1]
    for c, send_ref in enumerate(send_refs):
        for z in range(send_ref.shape[0]):
            send = acc[2 * z + 1 - core, c * rows : (c + 1) * rows]
            send_ref[z] = send.astype(BF16)


def gather_near(parts, me, tgt, far, got, tile):
    pieces, rows, width = far.shape
    return pl.pallas_call(
        functools.partial(gather_kernel, parts, tile),
        out_shape=[
            jax.ShapeDtypeStruct(far.shape, F32),
        ]
        + [jax.ShapeDtypeStruct((pieces // 2, rows // HALVES, width), BF16)] * HALVES,
        in_specs=[SMEM] * 2 + [VMEM] * (1 + len(got)),
        out_specs=[VMEM] * (1 + HALVES),
        input_output_aliases={2: 0},
        compiler_params=pltpu.CompilerParams(vmem_limit_bytes=16 * 2**20),
    )(me, tgt, far, *got)


def split_kernel(half, masks, me_ref, acc_ref, got_ref, *out_refs):
    z, core = me_ref[0] // 2, me_ref[0] % 2
    rows = got_ref.shape[1]
    for m, out_ref in zip(masks, out_refs):
        here = acc_ref[2 * (z ^ m) + core, half * rows : (half + 1) * rows]
        out_ref[...] = (here + got_ref[z ^ m].astype(F32)).astype(out_ref.dtype)


def split(half, masks, dtypes, me, acc, got):
    return pl.pallas_call(
        functools.partial(split_kernel, half, masks),
        out_shape=[jax.ShapeDtypeStruct(got.shape[1:], d) for d in dtypes],
        in_specs=[SMEM, VMEM, VMEM],
        out_specs=[VMEM] * len(masks),
        compiler_params=pltpu.CompilerParams(vmem_limit_bytes=16 * 2**20),
    )(me, acc, got)


def place_kernel(masks, me_ref, *refs):
    piece_refs, (out_ref, sems) = refs[: len(masks)], refs[-2:]
    copies = []
    for n, ((half, m), piece_ref) in enumerate(zip(masks, piece_refs)):
        rows, width = piece_ref.shape
        spot = pl.ds(pl.multiple_of((me_ref[0] ^ m) * width, width), width)
        out = out_ref.at[pl.ds(half * rows, rows), spot]
        copies.append(pltpu.make_async_copy(piece_ref, out, sems.at[n]))
    for copy in copies:
        copy.start()
    for copy in copies:
        copy.wait()


def place(masks, me, parts, count, out, early):
    rows, width = parts[0].shape
    return pl.pallas_call(
        functools.partial(place_kernel, masks),
        out_shape=jax.ShapeDtypeStruct((HALVES * rows, width * count), BF16),
        in_specs=[SMEM] + [VMEM] * len(parts) + [ANY] * (out is not None),
        out_specs=ANY,
        scratch_shapes=[pltpu.SemaphoreType.DMA((len(parts),))],
        input_output_aliases={} if out is None else {len(parts) + 1: 0},
        cost_estimate=LONG if early else None,
        compiler_params=pltpu.CompilerParams(vmem_limit_bytes=16 * 2**20),
    )(me, *parts, *(() if out is None else (out,)))


def swap(value, axis, mask):
    size = lax.axis_size(axis)
    return lax.ppermute(value, axis, [(i, i ^ mask) for i in range(size)])


def tied(value, *others):
    return lax.optimization_barrier((value,) + others)[0]


def begin_sums(half, me, acc, got):
    first, near, cross, own = split(half, (3, 1, 2, 0), (BF16, BF16, F32, F32), me, acc, got)
    a = swap(first, "src", 2)
    cross = (cross + a.astype(F32)).astype(BF16)
    return own, cross, swap(cross, "src", 4), swap(tied(near, cross), "src", 2)


def share(own, b, c):
    own = (own + b.astype(F32) + c.astype(F32)).astype(BF16)
    d = swap(own, "src", 4)
    return [own, swap(own, "src", 2), d, swap(d, "src", 2)]


def sums(me, acc, gots):
    chips = acc.shape[0] // 2
    masks = tuple(range(chips))
    if chips == 4:
        begun = [begin_sums(half, me, acc, got) for half, got in enumerate(gots)]
        shared = []
        for half, (own, _, b, c) in enumerate(begun):
            if half + 1 < len(begun):
                b = tied(b, begun[half + 1][1])
            shared.append(share(own, b, c))
        return masks, shared
    shared = []
    for half, got in enumerate(gots):
        dtypes = (F32,) + (BF16,) * (chips - 1)
        own, *rest = split(half, masks, dtypes, me, acc, got)
        for m, part in zip(masks[1:], rest):
            own = own + swap(part, "src", 2 * m).astype(F32)
        own = own.astype(BF16)
        shared.append([own] + [swap(own, "src", 2 * m) for m in masks[1:]])
    return masks, shared


def shards(
    charges, near_tiles, near_tgt, near_src, leaf_basis, transfer, coupling, far_node, target_basis
):
    groups = lax.axis_size("tgt")
    sources = lax.axis_size("src")
    me_t = lax.axis_index("tgt").astype(jnp.int32)
    me_s = lax.axis_index("src").astype(jnp.int32)
    count, tile, _ = near_tiles.shape
    slots = count // groups
    nrhs = charges.shape[1]
    x = charges.T
    me = me_t.reshape(1)

    masks = sorted(range(groups), key=lambda m: -bin(m).count("1"))
    ends = [min(FIRST_HEAD, slots)] + [min(HEAD, slots)] * (groups - 2) + [slots]
    heads = [Part(m, slots, 0, e, True) for m, e in zip(masks, ends)]
    tails = [Part(m, slots, e, slots, False) for m, e in zip(masks, ends) if e < slots]
    first = near_products(heads[:1], me, near_src, near_tgt, x, leaf_basis, near_tiles)
    rest = near_products(
        heads[1:] + tails, me, near_src, near_tgt, tied(x, *first), leaf_basis, near_tiles
    )
    parts = heads + tails
    got = {
        part: swap(y, "tgt", part.mask) if part.mask else y
        for part, y in zip(parts, [*first, *rest])
    }
    by_mask = {part.mask: got[part] for part in heads}

    rank = leaf_basis.shape[1]
    band = nrhs * rank // count

    def targets(some):
        rows = [by_mask[part.mask][::band, -rank:].reshape(1, count) for part in some]
        return jnp.concatenate(rows).astype(F32).astype(jnp.int32)

    early = [part for part in heads if part.mask in (masks[0], masks[-1])]
    late = [part for part in parts if part not in early]
    acc = start_near(
        early,
        me,
        targets(early),
        [got[part] for part in early],
        sources,
        target_basis.shape[0] // sources * tile,
        tile,
    )
    acc = far_field(
        me,
        far_node[0].reshape(-1),
        [by_mask[m] for m in range(groups)],
        transfer[0],
        coupling[0],
        target_basis,
        acc,
    )
    here = jnp.stack([me_t, me_s])
    acc, *sends = gather_near(
        late, here, targets(late), acc, [got[part] for part in late], tile
    )
    me = me_s.reshape(1)
    parts = []
    owners, shared = sums(me, acc, [swap(send, "src", 1) for send in sends])
    for half, mine in enumerate(shared):
        parts += [((half, 2 * m), q) for m, q in zip(owners, mine)]
        parts += [((half, 2 * m + 1), swap(q, "src", 1)) for m, q in zip(owners, mine)]
    last = parts[-len(owners) - 1], parts[-1]
    each = 2 * len(owners)
    steps = [parts[:-each], [part for part in parts[-each:] if part[0] not in dict(last)], last]
    out = None
    for some in steps:
        spots, values = zip(*some)
        out = place(spots, me, values, sources, out, some is not last)
    return out.T


def solution(mesh):
    in_specs = (
        P(("src", "tgt"), None),
        P(("src", "tgt"), None, None),
        P(("src", "tgt")),
        P(("src", "tgt")),
        P(("src", "tgt"), None, None),
        P("src", None, None, None),
        P("src", "tgt", None, None),
        P("src", "tgt", None),
        P("tgt", None, None),
    )
    out_specs = P("tgt", None)
    return jax.shard_map(shards, mesh=mesh, in_specs=in_specs, out_specs=out_specs, check_vma=False)
```

```python
import functools
import typing

import jax
import jax.numpy as jnp
from jax import lax
from jax.experimental import pallas as pl
from jax.experimental.pallas import tpu as pltpu
from jax.sharding import PartitionSpec as P

STEP = 32
HEAD = 2
FIRST_HEAD = 32
FAR_PIECES = 4
HALVES = 2
NEAR_VMEM = 60
F32, BF16 = jnp.float32, jnp.bfloat16
NT = (((1,), (1,)), ((), ()))
SMEM = pl.BlockSpec(memory_space=pltpu.SMEM)
LONG = pl.CostEstimate(flops=2**36, bytes_accessed=2**24, transcendentals=0)
VMEM = pl.BlockSpec(memory_space=pltpu.VMEM)
ANY = pl.BlockSpec(memory_space=pl.ANY)


class Part(typing.NamedTuple):
    mask: int
    slots: int
    begin: int
    end: int
    head: bool


def near_kernel(parts, me_ref, src_ref, tgt_ref, x_hbm, basis_ref, tiles_ref, *refs):
    outs, (x_ref, basis, held, sems) = refs[: len(parts)], refs[len(parts) :]
    tile = held.shape[1]
    leaves, rank, _ = basis.shape
    nrhs = x_ref.shape[0]
    count = tiles_ref.shape[0]
    slots = parts[0].slots
    extra = [
        pltpu.make_async_copy(x_hbm, x_ref, sems.at[0]),
        pltpu.make_async_copy(basis_ref, basis, sems.at[1]),
    ]
    copies, spans, at = [], [], 0
    for part in parts:
        first = (me_ref[0] ^ part.mask) * slots
        for k in range(part.begin, part.end, STEP):
            size = min(STEP, part.end - k)
            spans.append((part, k, size, at))
            copies.append(
                pltpu.make_async_copy(
                    tiles_ref.at[pl.ds(first + k, size)],
                    held.at[pl.ds(at, size)],
                    sems.at[2 + len(copies)],
                )
            )
            at += size
    for copy in extra + copies:
        copy.start()
    for copy in extra:
        copy.wait()
    if any(part.head for part in parts):
        root = jnp.zeros((nrhs, rank), F32)
        for i in range(leaves):
            root += lax.dot_general(
                x_ref[:, i * tile : (i + 1) * tile], basis[i], NT, preferred_element_type=F32
            )
        tgt = tgt_ref[...].astype(F32).astype(BF16)
        rows = nrhs * rank // count
        tgt = [
            jnp.broadcast_to(tgt[:, i : i + rank], (rows, rank)) for i in range(0, count, rank)
        ]
        roots = jnp.concatenate([root.astype(BF16), jnp.concatenate(tgt, axis=0)], axis=1)
        for part, out in zip(parts, outs):
            if part.head:
                out[:, out.shape[1] - 2 * rank :] = roots
    for (part, begin, size, at), copy in zip(spans, copies):
        copy.wait()
        first = (me_ref[0] ^ part.mask) * slots
        out = outs[parts.index(part)]
        for k in range(size):
            leaf = src_ref[first + begin + k]
            x = x_ref[:, pl.ds(pl.multiple_of(leaf * tile, tile), tile)]
            y = lax.dot_general(x, held[at + k], NT, preferred_element_type=F32)
            spot = (begin - part.begin + k) * tile
            out[:, spot : spot + tile] = y.astype(BF16)


def near_products(parts, me, near_src, near_tgt, x, basis, tiles):
    count, tile, _ = tiles.shape
    nrhs, rank = x.shape[0], basis.shape[1]
    widths = [(p.end - p.begin) * tile + (2 * rank if p.head else 0) for p in parts]
    blocks = sum(-(-(p.end - p.begin) // STEP) for p in parts)
    return pl.pallas_call(
        functools.partial(near_kernel, parts),
        out_shape=[jax.ShapeDtypeStruct((nrhs, w), BF16) for w in widths],
        in_specs=[SMEM, SMEM, VMEM, ANY, ANY, ANY],
        out_specs=[VMEM] * len(widths),
        scratch_shapes=[
            pltpu.VMEM(x.shape, BF16),
            pltpu.VMEM(basis.shape, BF16),
            pltpu.VMEM((sum(p.end - p.begin for p in parts), tile, tile), BF16),
            pltpu.SemaphoreType.DMA((blocks + 2,)),
        ],
        compiler_params=pltpu.CompilerParams(vmem_limit_bytes=NEAR_VMEM * 2**20),
    )(me, near_src, near_tgt.reshape(1, count), x, basis, tiles)


def add_products(acc, tgt_ref, me, parts, got_refs, tile):
    leaves = acc.shape[2] // tile
    for n, (part, got_ref) in enumerate(zip(parts, got_refs)):
        for k in range(part.begin, part.end):
            leaf = tgt_ref[n, me * part.slots + k]
            piece = leaf // leaves
            spot = pl.ds(pl.multiple_of((leaf - piece * leaves) * tile, tile), tile)
            at = (k - part.begin) * tile
            got = got_ref[:, at : at + tile].astype(F32)
            acc[piece, :, spot] = acc[piece, :, spot] + got


def start_kernel(parts, tile, me_ref, tgt_ref, *refs):
    acc = refs[-1]
    acc[...] = jnp.zeros_like(acc)
    add_products(acc, tgt_ref, me_ref[0], parts, refs[:-1], tile)


def start_near(parts, me, tgt, got, pieces, width, tile):
    return pl.pallas_call(
        functools.partial(start_kernel, parts, tile),
        out_shape=jax.ShapeDtypeStruct((pieces, got[0].shape[0], width), F32),
        in_specs=[SMEM, SMEM] + [VMEM] * len(got),
        out_specs=VMEM,
        cost_estimate=LONG,
        compiler_params=pltpu.CompilerParams(vmem_limit_bytes=16 * 2**20),
    )(me, tgt, *got)


def far_kernel(groups, me_ref, node_ref, *refs):
    head_refs = refs[:groups]
    edge_ref, coupling_ref, basis_ref, near_ref, out_ref, exact, low, high = refs[groups:]
    tgt_tiles, rank, tile = basis_ref.shape
    per = coupling_ref.shape[2] // rank
    pieces, nrhs, width = out_ref.shape
    leaves = width // tile
    for m in range(groups):
        end = head_refs[m].shape[1] - 2 * rank
        exact[groups - 1 + (me_ref[0] ^ m)] = head_refs[m][:, end : end + rank].astype(F32)
    for n in range(groups - 2, -1, -1):
        pair = jnp.concatenate([exact[2 * n + 1], exact[2 * n + 2]], axis=1)
        exact[n] = lax.dot_general(
            pair, edge_ref[n], NT, precision=lax.Precision.HIGHEST, preferred_element_type=F32
        )
    zero = jnp.zeros((nrhs, rank), BF16)
    for n in range(2 * groups - 1):
        node = exact[n].astype(BF16)
        low[n] = jnp.concatenate([node, zero], axis=1)
        high[n] = jnp.concatenate([zero, node], axis=1)

    @pl.loop(0, pieces // FAR_PIECES)
    def _(block):
        first = block * FAR_PIECES
        zs = []
        for i in range(FAR_PIECES * leaves):
            tau = first * leaves + i
            nodes = [node_ref[tau * per + k] for k in range(per)]
            stacked = jnp.concatenate(
                [low[nodes[k]] + high[nodes[k + 1]] for k in range(0, per, 2)], axis=1
            )
            z = lax.dot_general(stacked, coupling_ref[tau], NT, preferred_element_type=F32)
            zs.append(z.astype(BF16))
        for i in range(FAR_PIECES * leaves):
            far = jnp.dot(zs[i], basis_ref[first * leaves + i], preferred_element_type=F32)
            p, at = first + i // leaves, slice(i % leaves * tile, (i % leaves + 1) * tile)
            out_ref[p, :, at] = near_ref[p, :, at] + far


def far_field(me, far_node, heads, transfer, coupling, target_basis, near):
    groups = len(heads)
    rank = target_basis.shape[1]
    nrhs = near.shape[1]
    nodes = 2 * groups - 1
    return pl.pallas_call(
        functools.partial(far_kernel, groups),
        out_shape=jax.ShapeDtypeStruct(near.shape, F32),
        in_specs=[SMEM, SMEM] + [VMEM] * (groups + 4),
        out_specs=VMEM,
        scratch_shapes=[
            pltpu.VMEM((nodes, nrhs, rank), F32),
            pltpu.VMEM((nodes, nrhs, 2 * rank), BF16),
            pltpu.VMEM((nodes, nrhs, 2 * rank), BF16),
        ],
        input_output_aliases={groups + 5: 0},
        compiler_params=pltpu.CompilerParams(vmem_limit_bytes=16 * 2**20),
    )(me, far_node, *heads, transfer, coupling, target_basis, near)


def gather_kernel(parts, tile, me_ref, tgt_ref, far_ref, *refs):
    got_refs, acc, send_refs = refs[: len(parts)], refs[len(parts)], refs[len(parts) + 1 :]
    add_products(acc, tgt_ref, me_ref[0], parts, got_refs, tile)
    core = me_ref[1] % 2
    rows = send_refs[0].shape[1]
    for c, send_ref in enumerate(send_refs):
        for z in range(send_ref.shape[0]):
            send = acc[2 * z + 1 - core, c * rows : (c + 1) * rows]
            send_ref[z] = send.astype(BF16)


def gather_near(parts, me, tgt, far, got, tile):
    pieces, rows, width = far.shape
    return pl.pallas_call(
        functools.partial(gather_kernel, parts, tile),
        out_shape=[
            jax.ShapeDtypeStruct(far.shape, F32),
        ]
        + [jax.ShapeDtypeStruct((pieces // 2, rows // HALVES, width), BF16)] * HALVES,
        in_specs=[SMEM] * 2 + [VMEM] * (1 + len(got)),
        out_specs=[VMEM] * (1 + HALVES),
        input_output_aliases={2: 0},
        compiler_params=pltpu.CompilerParams(vmem_limit_bytes=16 * 2**20),
    )(me, tgt, far, *got)


def split_kernel(half, masks, me_ref, acc_ref, got_ref, *out_refs):
    z, core = me_ref[0] // 2, me_ref[0] % 2
    rows = got_ref.shape[1]
    for m, out_ref in zip(masks, out_refs):
        here = acc_ref[2 * (z ^ m) + core, half * rows : (half + 1) * rows]
        out_ref[...] = (here + got_ref[z ^ m].astype(F32)).astype(out_ref.dtype)


def split(half, masks, dtypes, me, acc, got):
    return pl.pallas_call(
        functools.partial(split_kernel, half, masks),
        out_shape=[jax.ShapeDtypeStruct(got.shape[1:], d) for d in dtypes],
        in_specs=[SMEM, VMEM, VMEM],
        out_specs=[VMEM] * len(masks),
        compiler_params=pltpu.CompilerParams(vmem_limit_bytes=16 * 2**20),
    )(me, acc, got)


def place_kernel(masks, me_ref, *refs):
    piece_refs, (out_ref, sems) = refs[: len(masks)], refs[-2:]
    copies = []
    for n, ((half, m), piece_ref) in enumerate(zip(masks, piece_refs)):
        rows, width = piece_ref.shape
        spot = pl.ds(pl.multiple_of((me_ref[0] ^ m) * width, width), width)
        out = out_ref.at[pl.ds(half * rows, rows), spot]
        copies.append(pltpu.make_async_copy(piece_ref, out, sems.at[n]))
    for copy in copies:
        copy.start()
    for copy in copies:
        copy.wait()


def place(masks, me, parts, count, out, early):
    rows, width = parts[0].shape
    return pl.pallas_call(
        functools.partial(place_kernel, masks),
        out_shape=jax.ShapeDtypeStruct((HALVES * rows, width * count), BF16),
        in_specs=[SMEM] + [VMEM] * len(parts) + [ANY] * (out is not None),
        out_specs=ANY,
        scratch_shapes=[pltpu.SemaphoreType.DMA((len(parts),))],
        input_output_aliases={} if out is None else {len(parts) + 1: 0},
        cost_estimate=LONG if early else None,
        compiler_params=pltpu.CompilerParams(vmem_limit_bytes=16 * 2**20),
    )(me, *parts, *(() if out is None else (out,)))


def swap(value, axis, mask):
    size = lax.axis_size(axis)
    return lax.ppermute(value, axis, [(i, i ^ mask) for i in range(size)])


def tied(value, *others):
    return lax.optimization_barrier((value,) + others)[0]


def begin_sums(half, me, acc, got):
    first, near, cross, own = split(half, (3, 1, 2, 0), (BF16, BF16, F32, F32), me, acc, got)
    a = swap(first, "src", 2)
    cross = (cross + a.astype(F32)).astype(BF16)
    return own, cross, swap(cross, "src", 4), swap(tied(near, cross), "src", 2)


def share(own, b, c):
    own = (own + b.astype(F32) + c.astype(F32)).astype(BF16)
    d = swap(own, "src", 4)
    return [own, swap(own, "src", 2), d, swap(d, "src", 2)]


def sums(me, acc, gots):
    chips = acc.shape[0] // 2
    masks = tuple(range(chips))
    if chips == 4:
        begun = [begin_sums(half, me, acc, got) for half, got in enumerate(gots)]
        shared = []
        for half, (own, _, b, c) in enumerate(begun):
            if half + 1 < len(begun):
                b = tied(b, begun[half + 1][1])
            shared.append(share(own, b, c))
        return masks, shared
    shared = []
    for half, got in enumerate(gots):
        dtypes = (F32,) + (BF16,) * (chips - 1)
        own, *rest = split(half, masks, dtypes, me, acc, got)
        for m, part in zip(masks[1:], rest):
            own = own + swap(part, "src", 2 * m).astype(F32)
        own = own.astype(BF16)
        shared.append([own] + [swap(own, "src", 2 * m) for m in masks[1:]])
    return masks, shared


def shards(
    charges, near_tiles, near_tgt, near_src, leaf_basis, transfer, coupling, far_node, target_basis
):
    groups = lax.axis_size("tgt")
    sources = lax.axis_size("src")
    me_t = lax.axis_index("tgt").astype(jnp.int32)
    me_s = lax.axis_index("src").astype(jnp.int32)
    count, tile, _ = near_tiles.shape
    slots = count // groups
    nrhs = charges.shape[1]
    x = charges.T
    me = me_t.reshape(1)

    masks = sorted(range(groups), key=lambda m: -bin(m).count("1"))
    ends = [min(FIRST_HEAD, slots)] + [min(HEAD, slots)] * (groups - 2) + [slots]
    heads = [Part(m, slots, 0, e, True) for m, e in zip(masks, ends)]
    tails = [Part(m, slots, e, slots, False) for m, e in zip(masks, ends) if e < slots]
    first = near_products(heads[:1], me, near_src, near_tgt, x, leaf_basis, near_tiles)
    rest = near_products(
        heads[1:] + tails, me, near_src, near_tgt, tied(x, *first), leaf_basis, near_tiles
    )
    parts = heads + tails
    got = {
        part: swap(y, "tgt", part.mask) if part.mask else y
        for part, y in zip(parts, [*first, *rest])
    }
    by_mask = {part.mask: got[part] for part in heads}

    rank = leaf_basis.shape[1]
    band = nrhs * rank // count

    def targets(some):
        rows = [by_mask[part.mask][::band, -rank:].reshape(1, count) for part in some]
        return jnp.concatenate(rows).astype(F32).astype(jnp.int32)

    early = [part for part in heads if part.mask in (masks[0], masks[-1])]
    late = [part for part in parts if part not in early]
    acc = start_near(
        early,
        me,
        targets(early),
        [got[part] for part in early],
        sources,
        target_basis.shape[0] // sources * tile,
        tile,
    )
    acc = far_field(
        me,
        far_node[0].reshape(-1),
        [by_mask[m] for m in range(groups)],
        transfer[0],
        coupling[0],
        target_basis,
        acc,
    )
    here = jnp.stack([me_t, me_s])
    acc, *sends = gather_near(
        late, here, targets(late), acc, [got[part] for part in late], tile
    )
    me = me_s.reshape(1)
    parts = []
    owners, shared = sums(me, acc, [swap(send, "src", 1) for send in sends])
    for half, mine in enumerate(shared):
        parts += [((half, 2 * m), q) for m, q in zip(owners, mine)]
        parts += [((half, 2 * m + 1), swap(q, "src", 1)) for m, q in zip(owners, mine)]
    last = parts[-len(owners) - 1], parts[-1]
    each = 2 * len(owners)
    steps = [parts[:-each], [part for part in parts[-each:] if part[0] not in dict(last)], last]
    out = None
    for some in steps:
        spots, values = zip(*some)
        out = place(spots, me, values, sources, out, some is not last)
    return out.T


def solution(mesh):
    in_specs = (
        P(("src", "tgt"), None),
        P(("src", "tgt"), None, None),
        P(("src", "tgt")),
        P(("src", "tgt")),
        P(("src", "tgt"), None, None),
        P("src", None, None, None),
        P("src", "tgt", None, None),
        P("src", "tgt", None),
        P("tgt", None, None),
    )
    out_specs = P("tgt", None)
    return jax.shard_map(shards, mesh=mesh, in_specs=in_specs, out_specs=out_specs, check_vma=False)
```
